32 devices in a mesh: spin: 2 (over core), band: 16 (over z, y, x).
Axes of the slice: x: 2, y: 2, z: 4, core: 2. Of those that a mesh axis runs over, the one named last changes fastest.
Arguments:
- orbitals: bfloat16 [128, 512000], P(('spin', 'band')), parts along dimension 0, may hold values from -40 to 40
Outputs:
- projector: float32 [32, 512000], P('spin', 'band'), parts along dimension 0
The draws below stay inside these ranges and needn't reach their ends.
There are 2 independent parts, one for each index of `spin`. The reference program is written for one: setup_inputs(seed, part) draws one part's arguments, and reference() takes and returns one part's arrays. A program takes and returns all parts, laid end to end along the dimension named above; each array names one. Nothing has to cross between parts.
All inputs are finite; a program needn't handle non-finite values.
Results may differ from the reference program's by a relative error of at most 0.0003.
Values may be sent and summed in bfloat16 or wider, within the bound.
A program may use at most 512 MiB of HBM per device.

```python
import math
import jax
import jax.numpy as jnp
from jax import lax

NG = 80
OWN = 4
NP = 2
NB = 64
N_BAND = 16


def draw_orbitals(key, part):
    total = NG ** 3
    common_key = jax.random.fold_in(key, 11)
    single_key = jax.random.fold_in(key, 12)
    scale_key = jax.random.fold_in(key, 13)
    planes = (jnp.arange(total, dtype=jnp.int32) // (NG * NG)).astype(jnp.float32) / NG
    common = jax.random.truncated_normal(common_key, -4.0, 4.0, (total,), jnp.float32)
    single = jax.random.truncated_normal(single_key, -4.0, 4.0, (NB, total), jnp.float32)
    amplitude = jnp.exp(jax.random.uniform(scale_key, (NB,), jnp.float32, math.log(0.5), math.log(2.0)))
    envelope = jnp.exp(0.55 * planes)
    values = amplitude[:, None] * envelope[None, :] * (0.7 * common[None, :] + single)
    return values.astype(jnp.bfloat16)


def setup_inputs(seed: int = 0, part: int = 0) -> dict:
    splits = jax.random.split(jax.random.key(seed), 2)
    part_keys = jax.random.split(jax.random.fold_in(splits[1], part), 2)
    return {
        "orbitals": draw_orbitals(jax.random.fold_in(jax.random.fold_in(splits[1], part), 71), part),
    }


def reference(orbitals):
    total = NG ** 3
    stride = N_BAND // NP
    grouped = orbitals.reshape(N_BAND, OWN, total)
    targets = grouped[:, 0].astype(jnp.float32)
    partners = grouped[::stride, OWN - 1].astype(jnp.float32)
    indices = jnp.arange(NG, dtype=jnp.int32)
    folded = jnp.minimum(indices, NG - indices).astype(jnp.float32)
    wavenumber = 2.0 * jnp.pi / NG * folded
    squares = wavenumber * wavenumber
    nyquist = NG // 2 + 1
    totals = squares[:, None, None] + squares[None, :, None] + squares[None, None, :nyquist]
    kernel = jnp.where(totals > 0.0, 1.0 / (0.0025 + totals), 0.0)

    def one_target(target):
        densities = (target[None, :] * partners).reshape(NP, NG, NG, NG)
        spectrum = jnp.fft.rfftn(densities, axes=(1, 2, 3))
        potential = jnp.fft.irfftn(spectrum * kernel, s=(NG, NG, NG), axes=(1, 2, 3))
        return -jnp.sum(partners * potential.reshape(NP, total), axis=0)
    vectors = lax.map(one_target, targets)
    intersection = jnp.dot(targets, vectors.T, precision=lax.Precision.HIGHEST) / total
    metric = -0.5 * (intersection + intersection.T)
    factor = jnp.linalg.cholesky(metric)
    return jax.scipy.linalg.solve_triangular(factor, vectors, lower=True)
```

```python
import functools

import jax
import jax.numpy as jnp
import numpy as np
from jax import lax
from jax.experimental import pallas as pl
from jax.experimental.pallas import tpu as pltpu
from jax.sharding import PartitionSpec as P

NG = 80
NP = 2
PAD = 128
QUARTERS = 4
highest = lax.Precision.HIGHEST


def tables(length):
    indices = np.arange(length)
    nyquist = length // 2
    frequency = np.where(indices <= nyquist, indices, indices - nyquist)
    angles = 2.0 * np.pi / length * (frequency[:, None] * indices[None, :] % length)
    edges = (indices == 0) | (indices == nyquist)
    weights = np.where(edges, 1.0 / length, 2.0 / length)
    fourier = np.where((indices <= nyquist)[:, None], np.cos(angles), np.sin(angles))
    fourier = (fourier * np.sqrt(weights)[:, None]).astype(np.float32)
    squares = ((2.0 * np.pi / length * frequency) ** 2).astype(np.float32)
    return fourier, squares


def halves(table):
    high = table.astype(jnp.bfloat16)
    low = (table - high.astype(np.float32)).astype(jnp.bfloat16)
    return high, low


def left_table(table):
    high, low = halves(table)
    return np.concatenate([high, high, low], axis=1)


def right_table(table, depth):
    high, low = halves(table)
    result = np.zeros((depth, 2 * PAD), dtype=high.dtype)
    result[: table.shape[0], : table.shape[1]] = high
    result[: table.shape[0], PAD : PAD + table.shape[1]] = low
    return result


def barrier_all(me, count):
    barrier = pltpu.get_barrier_semaphore()
    for step in range(1, count):
        pl.semaphore_signal(
            barrier, inc=1, device_id={"band": lax.rem(me + step, count)},
            device_id_type=pl.DeviceIdType.MESH,
        )
    pl.semaphore_wait(barrier, count - 1)


def remote(source, target, send, receive, device):
    return pltpu.make_async_remote_copy(
        src_ref=source, dst_ref=target, send_sem=send, recv_sem=receive,
        device_id={"band": device}, device_id_type=pl.DeviceIdType.MESH,
    )


def share_kernel(count, row, slabs, partners, gathered, first_send, column_send, plane_send,
                 receive, own_sem, slab_send, slab_receive, slab_own):
    me = lax.axis_index("band")
    planes = count // QUARTERS
    stride = count // NP
    column = lax.rem(me, QUARTERS)
    plane = lax.div(me, QUARTERS)
    base = plane * QUARTERS
    barrier_all(me, count)

    def first(r, q):
        return remote(row.at[q], partners.at[r, q], first_send.at[r, q - 1],
                      receive.at[r, q], lax.rem(me + q, count))

    def down(r, step):
        other = lax.rem(me + step * QUARTERS, count)
        return remote(partners.at[r, column], partners.at[r, column],
                      column_send.at[r, step - 1], receive.at[r, column], other)

    def across(r, step):
        other = base + lax.rem(column + step, QUARTERS)
        return remote(partners.at[r, column], partners.at[r, column],
                      plane_send.at[r, step - 1], receive.at[r, column], other)

    def slab(step):
        other = lax.rem(me + step, count)
        return remote(slabs.at[other], gathered.at[me], slab_send.at[step - 1],
                      slab_receive.at[step - 1], other)

    def arrived(r, q):
        remote(partners.at[r, q], partners.at[r, q], plane_send.at[r, 0],
               receive.at[r, q], me).wait_recv()

    for r in range(NP):
        @pl.when(me == r * stride)
        def _():
            for q in range(1, QUARTERS):
                first(r, q).start()
            own = pltpu.make_async_copy(row.at[0], partners.at[r, 0], own_sem)
            own.start()
            own.wait()

    for r in range(NP):
        @pl.when(me != r * stride)
        def _():
            arrived(r, column)

        @pl.when(plane == r * stride // QUARTERS)
        def _():
            for step in range(1, planes):
                down(r, step).start()

        for step in range(1, QUARTERS):
            across(r, step).start()

    mine = pltpu.make_async_copy(slabs.at[me], gathered.at[me], slab_own)
    mine.start()
    for step in range(1, count):
        slab(step).start()

    for r in range(NP):
        for step in range(1, QUARTERS):
            arrived(r, lax.rem(column + step, QUARTERS))
    for r in range(NP):
        @pl.when(me == r * stride)
        def _():
            for q in range(1, QUARTERS):
                first(r, q).wait_send()

        @pl.when(plane == r * stride // QUARTERS)
        def _():
            for step in range(1, planes):
                down(r, step).wait_send()

        for step in range(1, QUARTERS):
            across(r, step).wait_send()
    mine.wait()
    for step in range(1, count):
        slab(step).wait()


def share(row, slabs, count):
    planes = count // QUARTERS
    anywhere = pl.BlockSpec(memory_space=pl.ANY)
    dma = pltpu.SemaphoreType.DMA
    return pl.pallas_call(
        functools.partial(share_kernel, count),
        out_shape=(
            jax.ShapeDtypeStruct((NP,) + row.shape, row.dtype),
            jax.ShapeDtypeStruct(slabs.shape, slabs.dtype),
        ),
        in_specs=[anywhere] * 2,
        out_specs=(anywhere, anywhere),
        scratch_shapes=[
            dma((NP, QUARTERS - 1)), dma((NP, planes - 1)), dma((NP, QUARTERS - 1)),
            dma((NP, QUARTERS)), dma, dma((count - 1,)), dma((count - 1,)), dma,
        ],
        compiler_params=pltpu.CompilerParams(
            collective_id=0, has_side_effects=True, vmem_limit_bytes=1 << 20
        ),
        name="share",
    )(row, slabs)


def sum_kernel(count, part, total, held, send, receive):
    me = lax.axis_index("band")
    barrier_all(me, count)

    def copy(step):
        return remote(part, held.at[step], send.at[step], receive.at[step],
                      lax.rem(me + step, count))

    for step in range(1, count):
        copy(step).start()
    held[0] = part[...]
    for step in range(1, count):
        copy(step).wait()
    total[...] = jnp.sum(held[...], axis=0)


def sum_all(part, count):
    rows, columns = part.shape
    width = -(-columns // PAD) * PAD
    padded = jnp.pad(part, ((0, 0), (0, width - columns)))
    vmem = pl.BlockSpec(memory_space=pltpu.VMEM)
    total = pl.pallas_call(
        functools.partial(sum_kernel, count),
        out_shape=jax.ShapeDtypeStruct((rows, width), jnp.float32),
        in_specs=[vmem],
        out_specs=vmem,
        scratch_shapes=[
            pltpu.VMEM((count, rows, width), jnp.float32),
            pltpu.SemaphoreType.DMA((count,)),
            pltpu.SemaphoreType.DMA((count,)),
        ],
        compiler_params=pltpu.CompilerParams(collective_id=1, has_side_effects=True),
        name="sum_all",
    )(padded)
    return total[:, :columns]


def split(values):
    high = values.astype(jnp.bfloat16)
    low = (values - high.astype(jnp.float32)).astype(jnp.bfloat16)
    return high, low


def dot(left, right):
    return lax.dot_general(left, right, (((1,), (0,)), ((), ())),
                           preferred_element_type=jnp.float32)


def from_left(table, values):
    high, low = split(values)
    return dot(table, jnp.concatenate([high, low, high], axis=0))


def from_right(values, table):
    high, low = split(values)
    both = dot(high, table)
    return both[:, :PAD] + both[:, PAD:] + dot(low, table[:, :PAD])


def exchange_kernel(target, partners, forward_left, inverse_left, forward_right, inverse_right,
                    row_squares, lane_squares, vectors, one, two):
    group = 8

    def ahead(step, carry):
        planes = pl.ds(step * group, group)
        left = target[planes].astype(jnp.float32)
        parts = []
        for r in range(NP):
            density = left * partners[r, planes].astype(jnp.float32)
            parts.append(from_right(density.reshape(group * NG, NG), forward_right[...]))
        values = jnp.concatenate(parts, axis=1).reshape(group, NG, NP * PAD)
        out = jnp.stack([from_left(forward_left[...], values[i]) for i in range(group)])
        one[:, pl.ds(pl.multiple_of(step * group, group), group), :] = jnp.swapaxes(out, 0, 1)
        return carry

    lax.fori_loop(0, NG // group, ahead, 0)

    def middle(step, carry):
        outs = []
        for i in range(group):
            number = step * group + i
            folded = jnp.where(number <= NG // 2, number, number - NG // 2)
            wave = (2.0 * np.pi / NG) * folded.astype(jnp.float32)
            totals = row_squares[...] + lane_squares[...] + wave * wave
            weight = jnp.where(totals > 0.0, 1.0 / (0.0025 + totals), 0.0)
            spectrum = from_left(forward_left[...], one[number]) * weight
            outs.append(from_left(inverse_left[...], spectrum))
        out = jnp.stack(outs)
        two[:, pl.ds(pl.multiple_of(step * group, group), group), :] = jnp.swapaxes(out, 0, 1)
        return carry

    lax.fori_loop(0, NG // group, middle, 0)

    def back(step, carry):
        planes = pl.ds(step * group, group)
        values = jnp.stack(
            [from_left(inverse_left[...], two[step * group + i]) for i in range(group)]
        ).reshape(group * NG, NP * PAD)
        total = jnp.zeros((group, NG, NG), jnp.float32)
        for r in range(NP):
            potential = from_right(values[:, r * PAD : (r + 1) * PAD], inverse_right[...])
            potential = potential.reshape(group, NG, PAD)[:, :, :NG]
            total -= partners[r, planes].astype(jnp.float32) * potential
        vectors[planes] = total
        return carry

    lax.fori_loop(0, NG // group, back, 0)


def exchange(target, partners):
    fourier, squares = tables(NG)
    lanes = np.zeros((PAD,), np.float32)
    lanes[:NG] = squares
    vmem = pl.BlockSpec(memory_space=pltpu.VMEM)
    return pl.pallas_call(
        exchange_kernel,
        out_shape=jax.ShapeDtypeStruct((NG, NG, NG), jnp.float32),
        in_specs=[vmem] * 8,
        out_specs=vmem,
        scratch_shapes=[pltpu.VMEM((NG, NG, NP * PAD), jnp.float32)] * 2,
        compiler_params=pltpu.CompilerParams(vmem_limit_bytes=48 << 20),
        cost_estimate=pl.CostEstimate(
            flops=12 * NP * NG**4, bytes_accessed=8 << 20, transcendentals=0
        ),
        name="exchange",
    )(
        target,
        partners,
        left_table(fourier),
        left_table(fourier.T.copy()),
        right_table(fourier.T.copy(), NG),
        right_table(fourier, PAD),
        np.broadcast_to(squares[:, None], (NG, NP * PAD)).copy(),
        np.tile(lanes, NP)[None, :],
    )


def body(orbitals):
    devices = lax.axis_size("band")
    owned_rows = orbitals.shape[0]
    points = orbitals.shape[1]
    target = orbitals[0]
    row = orbitals[owned_rows - 1].reshape(QUARTERS, points // QUARTERS // PAD, PAD)
    slabs = target.reshape(devices, 8, points // devices // 8)
    partners, target_slab = share(row, slabs, devices)
    vectors = exchange(target.reshape(NG, NG, NG), partners.reshape(NP, NG, NG, NG))
    vector_slab = lax.all_to_all(
        vectors.reshape(1, points), "band", split_axis=1, concat_axis=0, tiled=True
    )
    target_slab = target_slab.reshape(devices, points // devices).astype(jnp.float32)
    part = jnp.einsum("ap,bp->ab", target_slab, vector_slab, precision=highest) / NG**3
    intersection = sum_all(part, devices)
    metric = -0.5 * (intersection + intersection.T)
    factor = jnp.linalg.cholesky(metric)
    return jax.scipy.linalg.solve_triangular(factor, vector_slab, lower=True)


def solution(mesh):
    placed = (P(("spin", "band"), None),)
    return jax.shard_map(
        body, mesh=mesh, in_specs=placed, out_specs=P("spin", "band"), check_vma=False
    )
```

```python
import functools

import jax
import jax.numpy as jnp
import numpy as np
from jax import lax
from jax.experimental import pallas as pl
from jax.experimental.pallas import tpu as pltpu
from jax.sharding import PartitionSpec as P

NG = 80
NP = 2
PAD = 128
QUARTERS = 4
highest = lax.Precision.HIGHEST


def tables(length):
    indices = np.arange(length)
    nyquist = length // 2
    frequency = np.where(indices <= nyquist, indices, indices - nyquist)
    angles = 2.0 * np.pi / length * (frequency[:, None] * indices[None, :] % length)
    edges = (indices == 0) | (indices == nyquist)
    weights = np.where(edges, 1.0 / length, 2.0 / length)
    fourier = np.where((indices <= nyquist)[:, None], np.cos(angles), np.sin(angles))
    fourier = (fourier * np.sqrt(weights)[:, None]).astype(np.float32)
    squares = ((2.0 * np.pi / length * frequency) ** 2).astype(np.float32)
    return fourier, squares


def halves(table):
    high = table.astype(jnp.bfloat16)
    low = (table - high.astype(np.float32)).astype(jnp.bfloat16)
    return high, low


def left_table(table):
    high, low = halves(table)
    return np.concatenate([high, high, low], axis=1)


def right_table(table, depth):
    high, low = halves(table)
    result = np.zeros((depth, 2 * PAD), dtype=high.dtype)
    result[: table.shape[0], : table.shape[1]] = high
    result[: table.shape[0], PAD : PAD + table.shape[1]] = low
    return result


def barrier_all(me, count):
    barrier = pltpu.get_barrier_semaphore()
    for step in range(1, count):
        pl.semaphore_signal(
            barrier, inc=1, device_id={"band": lax.rem(me + step, count)},
            device_id_type=pl.DeviceIdType.MESH,
        )
    pl.semaphore_wait(barrier, count - 1)


def remote(source, target, send, receive, device):
    return pltpu.make_async_remote_copy(
        src_ref=source, dst_ref=target, send_sem=send, recv_sem=receive,
        device_id={"band": device}, device_id_type=pl.DeviceIdType.MESH,
    )


def share_kernel(count, row, partners, first_send, column_send, plane_send, receive, own_sem):
    me = lax.axis_index("band")
    planes = count // QUARTERS
    stride = count // NP
    column = lax.rem(me, QUARTERS)
    plane = lax.div(me, QUARTERS)
    base = plane * QUARTERS
    barrier_all(me, count)

    def first(r, q):
        return remote(row.at[q], partners.at[r, q], first_send.at[r, q - 1],
                      receive.at[r, q], lax.rem(me + q, count))

    def down(r, step):
        other = lax.rem(me + step * QUARTERS, count)
        return remote(partners.at[r, column], partners.at[r, column],
                      column_send.at[r, step - 1], receive.at[r, column], other)

    def across(r, step):
        other = base + lax.rem(column + step, QUARTERS)
        return remote(partners.at[r, column], partners.at[r, column],
                      plane_send.at[r, step - 1], receive.at[r, column], other)

    def arrived(r, q):
        remote(partners.at[r, q], partners.at[r, q], plane_send.at[r, 0],
               receive.at[r, q], me).wait_recv()

    for r in range(NP):
        @pl.when(me == r * stride)
        def _():
            for q in range(1, QUARTERS):
                first(r, q).start()
            own = pltpu.make_async_copy(row.at[0], partners.at[r, 0], own_sem)
            own.start()
            own.wait()

    for r in range(NP):
        @pl.when(me != r * stride)
        def _():
            arrived(r, column)

        @pl.when(plane == r * stride // QUARTERS)
        def _():
            for step in range(1, planes):
                down(r, step).start()

        for step in range(1, QUARTERS):
            across(r, step).start()

    for r in range(NP):
        for step in range(1, QUARTERS):
            arrived(r, lax.rem(column + step, QUARTERS))
    for r in range(NP):
        @pl.when(me == r * stride)
        def _():
            for q in range(1, QUARTERS):
                first(r, q).wait_send()

        @pl.when(plane == r * stride // QUARTERS)
        def _():
            for step in range(1, planes):
                down(r, step).wait_send()

        for step in range(1, QUARTERS):
            across(r, step).wait_send()


def share(row, count):
    planes = count // QUARTERS
    anywhere = pl.BlockSpec(memory_space=pl.ANY)
    dma = pltpu.SemaphoreType.DMA
    return pl.pallas_call(
        functools.partial(share_kernel, count),
        out_shape=jax.ShapeDtypeStruct((NP,) + row.shape, row.dtype),
        in_specs=[anywhere],
        out_specs=anywhere,
        scratch_shapes=[
            dma((NP, QUARTERS - 1)), dma((NP, planes - 1)), dma((NP, QUARTERS - 1)),
            dma((NP, QUARTERS)), dma,
        ],
        compiler_params=pltpu.CompilerParams(
            collective_id=0, has_side_effects=True, vmem_limit_bytes=1 << 20
        ),
        name="share",
    )(row)


def sum_kernel(count, part, total, held, send, receive):
    me = lax.axis_index("band")
    barrier_all(me, count)

    def copy(step):
        return remote(part, held.at[step], send.at[step], receive.at[step],
                      lax.rem(me + step, count))

    for step in range(1, count):
        copy(step).start()
    held[0] = part[...]
    for step in range(1, count):
        copy(step).wait()
    total[...] = jnp.sum(held[...], axis=0)


def sum_all(part, count):
    rows, columns = part.shape
    width = -(-columns // PAD) * PAD
    padded = jnp.pad(part, ((0, 0), (0, width - columns)))
    vmem = pl.BlockSpec(memory_space=pltpu.VMEM)
    total = pl.pallas_call(
        functools.partial(sum_kernel, count),
        out_shape=jax.ShapeDtypeStruct((rows, width), jnp.float32),
        in_specs=[vmem],
        out_specs=vmem,
        scratch_shapes=[
            pltpu.VMEM((count, rows, width), jnp.float32),
            pltpu.SemaphoreType.DMA((count,)),
            pltpu.SemaphoreType.DMA((count,)),
        ],
        compiler_params=pltpu.CompilerParams(collective_id=1, has_side_effects=True),
        name="sum_all",
    )(padded)
    return total[:, :columns]


def pick_kernel(orbitals, first, last):
    owned, width = orbitals.shape
    values = orbitals[...].astype(jnp.float32)
    first[...] = values[0:1].reshape(width // PAD, PAD).astype(first.dtype)
    last[...] = values[owned - 1 : owned].reshape(width // PAD, PAD).astype(last.dtype)


def pick(orbitals):
    owned, points = orbitals.shape
    steps = 10
    width = points // steps
    row = jax.ShapeDtypeStruct((points // PAD, PAD), orbitals.dtype)
    spec = pl.BlockSpec((width // PAD, PAD), lambda i: (i, 0))
    return pl.pallas_call(
        pick_kernel,
        grid=(steps,),
        out_shape=(row, row),
        in_specs=[pl.BlockSpec((owned, width), lambda i: (0, i))],
        out_specs=(spec, spec),
        compiler_params=pltpu.CompilerParams(vmem_limit_bytes=32 << 20),
        name="pick",
    )(orbitals)


def split(values):
    high = values.astype(jnp.bfloat16)
    low = (values - high.astype(jnp.float32)).astype(jnp.bfloat16)
    return high, low


def dot(left, right):
    return lax.dot_general(left, right, (((1,), (0,)), ((), ())),
                           preferred_element_type=jnp.float32)


def from_left(table, values):
    high, low = split(values)
    return dot(table, jnp.concatenate([high, low, high], axis=0))


def from_right(values, table):
    high, low = split(values)
    both = dot(high, table)
    return both[:, :PAD] + both[:, PAD:] + dot(low, table[:, :PAD])


def exchange_kernel(target, partners, forward_left, inverse_left, forward_right, inverse_right,
                    row_squares, lane_squares, vectors, one, two):
    group = 8

    def ahead(step, carry):
        planes = pl.ds(step * group, group)
        left = target[planes].astype(jnp.float32)
        parts = []
        for r in range(NP):
            density = left * partners[r, planes].astype(jnp.float32)
            parts.append(from_right(density.reshape(group * NG, NG), forward_right[...]))
        values = jnp.concatenate(parts, axis=1).reshape(group, NG, NP * PAD)
        out = jnp.stack([from_left(forward_left[...], values[i]) for i in range(group)])
        one[:, pl.ds(pl.multiple_of(step * group, group), group), :] = jnp.swapaxes(out, 0, 1)
        return carry

    lax.fori_loop(0, NG // group, ahead, 0)

    def middle(step, carry):
        outs = []
        for i in range(group):
            number = step * group + i
            folded = jnp.where(number <= NG // 2, number, number - NG // 2)
            wave = (2.0 * np.pi / NG) * folded.astype(jnp.float32)
            totals = row_squares[...] + lane_squares[...] + wave * wave
            weight = jnp.where(totals > 0.0, 1.0 / (0.0025 + totals), 0.0)
            spectrum = from_left(forward_left[...], one[number]) * weight
            outs.append(from_left(inverse_left[...], spectrum))
        out = jnp.stack(outs)
        two[:, pl.ds(pl.multiple_of(step * group, group), group), :] = jnp.swapaxes(out, 0, 1)
        return carry

    lax.fori_loop(0, NG // group, middle, 0)

    def back(step, carry):
        planes = pl.ds(step * group, group)
        values = jnp.stack(
            [from_left(inverse_left[...], two[step * group + i]) for i in range(group)]
        ).reshape(group * NG, NP * PAD)
        total = jnp.zeros((group, NG, NG), jnp.float32)
        for r in range(NP):
            potential = from_right(values[:, r * PAD : (r + 1) * PAD], inverse_right[...])
            potential = potential.reshape(group, NG, PAD)[:, :, :NG]
            total -= partners[r, planes].astype(jnp.float32) * potential
        vectors[planes] = total
        return carry

    lax.fori_loop(0, NG // group, back, 0)


def exchange(target, partners):
    fourier, squares = tables(NG)
    lanes = np.zeros((PAD,), np.float32)
    lanes[:NG] = squares
    vmem = pl.BlockSpec(memory_space=pltpu.VMEM)
    return pl.pallas_call(
        exchange_kernel,
        out_shape=jax.ShapeDtypeStruct((NG, NG, NG), jnp.float32),
        in_specs=[vmem] * 8,
        out_specs=vmem,
        scratch_shapes=[pltpu.VMEM((NG, NG, NP * PAD), jnp.float32)] * 2,
        compiler_params=pltpu.CompilerParams(vmem_limit_bytes=48 << 20),
        cost_estimate=pl.CostEstimate(
            flops=12 * NP * NG**4, bytes_accessed=8 << 20, transcendentals=0
        ),
        name="exchange",
    )(
        target,
        partners,
        left_table(fourier),
        left_table(fourier.T.copy()),
        right_table(fourier.T.copy(), NG),
        right_table(fourier, PAD),
        np.broadcast_to(squares[:, None], (NG, NP * PAD)).copy(),
        np.tile(lanes, NP)[None, :],
    )


def body(orbitals):
    devices = lax.axis_size("band")
    points = orbitals.shape[1]
    target, row = pick(orbitals)
    partners = share(row.reshape(QUARTERS, points // QUARTERS // PAD, PAD), devices)
    ready, partners = lax.optimization_barrier((target, partners))
    target_slab = lax.all_to_all(
        ready.reshape(1, points), "band", split_axis=1, concat_axis=0, tiled=True
    )
    vectors = exchange(target.reshape(NG, NG, NG), partners.reshape(NP, NG, NG, NG))
    vector_slab = lax.all_to_all(
        vectors.reshape(1, points), "band", split_axis=1, concat_axis=0, tiled=True
    )
    target_slab = target_slab.reshape(devices, points // devices).astype(jnp.float32)
    part = jnp.einsum("ap,bp->ab", target_slab, vector_slab, precision=highest) / NG**3
    intersection = sum_all(part, devices)
    metric = -0.5 * (intersection + intersection.T)
    factor = jnp.linalg.cholesky(metric)
    return jax.scipy.linalg.solve_triangular(factor, vector_slab, lower=True)


def solution(mesh):
    placed = (P(("spin", "band"), None),)
    return jax.shard_map(
        body, mesh=mesh, in_specs=placed, out_specs=P("spin", "band"), check_vma=False
    )
```

```python
import functools

import jax
import jax.numpy as jnp
import numpy as np
from jax import lax
from jax.experimental import pallas as pl
from jax.experimental.pallas import tpu as pltpu
from jax.sharding import PartitionSpec as P

NG = 80
NP = 2
PAD = 128
QUARTERS = 4
highest = lax.Precision.HIGHEST


def tables(length):
    indices = np.arange(length)
    nyquist = length // 2
    frequency = np.where(indices <= nyquist, indices, indices - nyquist)
    angles = 2.0 * np.pi / length * (frequency[:, None] * indices[None, :] % length)
    edges = (indices == 0) | (indices == nyquist)
    weights = np.where(edges, 1.0 / length, 2.0 / length)
    fourier = np.where((indices <= nyquist)[:, None], np.cos(angles), np.sin(angles))
    fourier = (fourier * np.sqrt(weights)[:, None]).astype(np.float32)
    squares = ((2.0 * np.pi / length * frequency) ** 2).astype(np.float32)
    return fourier, squares


def halves(table):
    high = table.astype(jnp.bfloat16)
    low = (table - high.astype(np.float32)).astype(jnp.bfloat16)
    return high, low


def left_table(table):
    high, low = halves(table)
    return np.concatenate([high, high, low], axis=1)


def right_table(table, depth):
    high, low = halves(table)
    result = np.zeros((depth, 2 * PAD), dtype=high.dtype)
    result[: table.shape[0], : table.shape[1]] = high
    result[: table.shape[0], PAD : PAD + table.shape[1]] = low
    return result


def barrier_all(me, count):
    barrier = pltpu.get_barrier_semaphore()
    for step in range(1, count):
        pl.semaphore_signal(
            barrier, inc=1, device_id={"band": lax.rem(me + step, count)},
            device_id_type=pl.DeviceIdType.MESH,
        )
    pl.semaphore_wait(barrier, count - 1)


def remote(source, target, send, receive, device):
    return pltpu.make_async_remote_copy(
        src_ref=source, dst_ref=target, send_sem=send, recv_sem=receive,
        device_id={"band": device}, device_id_type=pl.DeviceIdType.MESH,
    )


def share_kernel(count, row, partners, first_send, column_send, plane_send, receive, own_sem):
    me = lax.axis_index("band")
    planes = count // QUARTERS
    stride = count // NP
    column = lax.rem(me, QUARTERS)
    plane = lax.div(me, QUARTERS)
    base = plane * QUARTERS
    barrier_all(me, count)

    def first(r, q):
        return remote(row.at[q], partners.at[r, q], first_send.at[r, q - 1],
                      receive.at[r, q], lax.rem(me + q, count))

    def down(r, step):
        other = lax.rem(me + step * QUARTERS, count)
        return remote(partners.at[r, column], partners.at[r, column],
                      column_send.at[r, step - 1], receive.at[r, column], other)

    def across(r, step):
        other = base + lax.rem(column + step, QUARTERS)
        return remote(partners.at[r, column], partners.at[r, column],
                      plane_send.at[r, step - 1], receive.at[r, column], other)

    def arrived(r, q):
        remote(partners.at[r, q], partners.at[r, q], plane_send.at[r, 0],
               receive.at[r, q], me).wait_recv()

    for r in range(NP):
        @pl.when(me == r * stride)
        def _():
            for q in range(1, QUARTERS):
                first(r, q).start()
            own = pltpu.make_async_copy(row.at[0], partners.at[r, 0], own_sem)
            own.start()
            own.wait()

    for r in range(NP):
        @pl.when(me != r * stride)
        def _():
            arrived(r, column)

        @pl.when(plane == r * stride // QUARTERS)
        def _():
            for step in range(1, planes):
                down(r, step).start()

        for step in range(1, QUARTERS):
            across(r, step).start()

    for r in range(NP):
        for step in range(1, QUARTERS):
            arrived(r, lax.rem(column + step, QUARTERS))
    for r in range(NP):
        @pl.when(me == r * stride)
        def _():
            for q in range(1, QUARTERS):
                first(r, q).wait_send()

        @pl.when(plane == r * stride // QUARTERS)
        def _():
            for step in range(1, planes):
                down(r, step).wait_send()

        for step in range(1, QUARTERS):
            across(r, step).wait_send()


def share(row, count):
    planes = count // QUARTERS
    anywhere = pl.BlockSpec(memory_space=pl.ANY)
    dma = pltpu.SemaphoreType.DMA
    return pl.pallas_call(
        functools.partial(share_kernel, count),
        out_shape=jax.ShapeDtypeStruct((NP,) + row.shape, row.dtype),
        in_specs=[anywhere],
        out_specs=anywhere,
        scratch_shapes=[
            dma((NP, QUARTERS - 1)), dma((NP, planes - 1)), dma((NP, QUARTERS - 1)),
            dma((NP, QUARTERS)), dma,
        ],
        compiler_params=pltpu.CompilerParams(
            collective_id=0, has_side_effects=True, vmem_limit_bytes=1 << 20
        ),
        name="share",
    )(row)


def sum_kernel(count, part, total, held, send, receive):
    me = lax.axis_index("band")
    barrier_all(me, count)

    def copy(step):
        return remote(part, held.at[step], send.at[step], receive.at[step],
                      lax.rem(me + step, count))

    for step in range(1, count):
        copy(step).start()
    held[0] = part[...]
    for step in range(1, count):
        copy(step).wait()
    total[...] = jnp.sum(held[...], axis=0)


def sum_all(part, count):
    rows, columns = part.shape
    width = -(-columns // PAD) * PAD
    padded = jnp.pad(part, ((0, 0), (0, width - columns)))
    vmem = pl.BlockSpec(memory_space=pltpu.VMEM)
    total = pl.pallas_call(
        functools.partial(sum_kernel, count),
        out_shape=jax.ShapeDtypeStruct((rows, width), jnp.float32),
        in_specs=[vmem],
        out_specs=vmem,
        scratch_shapes=[
            pltpu.VMEM((count, rows, width), jnp.float32),
            pltpu.SemaphoreType.DMA((count,)),
            pltpu.SemaphoreType.DMA((count,)),
        ],
        compiler_params=pltpu.CompilerParams(collective_id=1, has_side_effects=True),
        name="sum_all",
    )(padded)
    return total[:, :columns]


def pick_kernel(orbitals, first, last):
    owned, width = orbitals.shape
    values = orbitals[...].astype(jnp.float32)
    first[...] = values[0:1].reshape(width // PAD, PAD).astype(first.dtype)
    last[...] = values[owned - 1 : owned].reshape(width // PAD, PAD).astype(last.dtype)


def pick(orbitals):
    owned, points = orbitals.shape
    steps = 10
    width = points // steps
    row = jax.ShapeDtypeStruct((points // PAD, PAD), orbitals.dtype)
    spec = pl.BlockSpec((width // PAD, PAD), lambda i: (i, 0))
    return pl.pallas_call(
        pick_kernel,
        grid=(steps,),
        out_shape=(row, row),
        in_specs=[pl.BlockSpec((owned, width), lambda i: (0, i))],
        out_specs=(spec, spec),
        compiler_params=pltpu.CompilerParams(vmem_limit_bytes=32 << 20),
        name="pick",
    )(orbitals)


def split(values):
    high = values.astype(jnp.bfloat16)
    low = (values - high.astype(jnp.float32)).astype(jnp.bfloat16)
    return high, low


def dot(left, right):
    return lax.dot_general(left, right, (((1,), (0,)), ((), ())),
                           preferred_element_type=jnp.float32)


def from_left(table, values):
    high, low = split(values)
    return dot(table, jnp.concatenate([high, low, high], axis=0))


def from_right(values, table):
    high, low = split(values)
    both = dot(high, table)
    return both[:, :PAD] + both[:, PAD:] + dot(low, table[:, :PAD])


def exchange_kernel(count, target, partners, forward_left, inverse_left, forward_right,
                    inverse_right, row_squares, lane_squares, slabs, vectors, gathered, one, two,
                    send, receive, own_sem):
    group = 8
    me = lax.axis_index("band")
    barrier_all(me, count)

    def slab(step):
        other = lax.rem(me + step, count)
        return remote(slabs.at[other], gathered.at[me], send.at[step], receive.at[step], other)

    for step in range(1, count):
        slab(step).start()
    own = pltpu.make_async_copy(slabs.at[me], gathered.at[me], own_sem)
    own.start()

    def ahead(step, carry):
        planes = pl.ds(step * group, group)
        left = target[planes].astype(jnp.float32)
        parts = []
        for r in range(NP):
            density = left * partners[r, planes].astype(jnp.float32)
            parts.append(from_right(density.reshape(group * NG, NG), forward_right[...]))
        values = jnp.concatenate(parts, axis=1).reshape(group, NG, NP * PAD)
        out = jnp.stack([from_left(forward_left[...], values[i]) for i in range(group)])
        one[:, pl.ds(pl.multiple_of(step * group, group), group), :] = jnp.swapaxes(out, 0, 1)
        return carry

    lax.fori_loop(0, NG // group, ahead, 0)

    def middle(step, carry):
        outs = []
        for i in range(group):
            number = step * group + i
            folded = jnp.where(number <= NG // 2, number, number - NG // 2)
            wave = (2.0 * np.pi / NG) * folded.astype(jnp.float32)
            totals = row_squares[...] + lane_squares[...] + wave * wave
            weight = jnp.where(totals > 0.0, 1.0 / (0.0025 + totals), 0.0)
            spectrum = from_left(forward_left[...], one[number]) * weight
            outs.append(from_left(inverse_left[...], spectrum))
        out = jnp.stack(outs)
        two[:, pl.ds(pl.multiple_of(step * group, group), group), :] = jnp.swapaxes(out, 0, 1)
        return carry

    lax.fori_loop(0, NG // group, middle, 0)

    def back(step, carry):
        planes = pl.ds(step * group, group)
        values = jnp.stack(
            [from_left(inverse_left[...], two[step * group + i]) for i in range(group)]
        ).reshape(group * NG, NP * PAD)
        total = jnp.zeros((group, NG, NG), jnp.float32)
        for r in range(NP):
            potential = from_right(values[:, r * PAD : (r + 1) * PAD], inverse_right[...])
            potential = potential.reshape(group, NG, PAD)[:, :, :NG]
            total -= partners[r, planes].astype(jnp.float32) * potential
        vectors[planes] = total
        return carry

    lax.fori_loop(0, NG // group, back, 0)
    own.wait()
    for step in range(1, count):
        slab(step).wait()


def exchange(target, partners, slabs, count):
    fourier, squares = tables(NG)
    lanes = np.zeros((PAD,), np.float32)
    lanes[:NG] = squares
    vmem = pl.BlockSpec(memory_space=pltpu.VMEM)
    anywhere = pl.BlockSpec(memory_space=pl.ANY)
    dma = pltpu.SemaphoreType.DMA
    return pl.pallas_call(
        functools.partial(exchange_kernel, count),
        out_shape=(
            jax.ShapeDtypeStruct((NG, NG, NG), jnp.float32),
            jax.ShapeDtypeStruct(slabs.shape, slabs.dtype),
        ),
        in_specs=[vmem] * 8 + [anywhere],
        out_specs=(vmem, anywhere),
        scratch_shapes=[pltpu.VMEM((NG, NG, NP * PAD), jnp.float32)] * 2
        + [dma((count,)), dma((count,)), dma],
        compiler_params=pltpu.CompilerParams(
            collective_id=2, has_side_effects=True, vmem_limit_bytes=48 << 20
        ),
        cost_estimate=pl.CostEstimate(
            flops=12 * NP * NG**4, bytes_accessed=8 << 20, transcendentals=0
        ),
        name="exchange",
    )(
        target,
        partners,
        left_table(fourier),
        left_table(fourier.T.copy()),
        right_table(fourier.T.copy(), NG),
        right_table(fourier, PAD),
        np.broadcast_to(squares[:, None], (NG, NP * PAD)).copy(),
        np.tile(lanes, NP)[None, :],
        slabs,
    )


def body(orbitals):
    devices = lax.axis_size("band")
    points = orbitals.shape[1]
    target, row = pick(orbitals)
    partners = share(row.reshape(QUARTERS, points // QUARTERS // PAD, PAD), devices)
    vectors, target_slab = exchange(
        target.reshape(NG, NG, NG),
        partners.reshape(NP, NG, NG, NG),
        target.reshape(devices, 8, points // devices // 8),
        devices,
    )
    vector_slab = lax.all_to_all(
        vectors.reshape(1, points), "band", split_axis=1, concat_axis=0, tiled=True
    )
    target_slab = target_slab.reshape(devices, points // devices).astype(jnp.float32)
    part = jnp.einsum("ap,bp->ab", target_slab, vector_slab, precision=highest) / NG**3
    intersection = sum_all(part, devices)
    metric = -0.5 * (intersection + intersection.T)
    factor = jnp.linalg.cholesky(metric)
    return jax.scipy.linalg.solve_triangular(factor, vector_slab, lower=True)


def solution(mesh):
    placed = (P(("spin", "band"), None),)
    return jax.shard_map(
        body, mesh=mesh, in_specs=placed, out_specs=P("spin", "band"), check_vma=False
    )
```

```python
import functools

import jax
import jax.numpy as jnp
import numpy as np
from jax import lax
from jax.experimental import pallas as pl
from jax.experimental.pallas import tpu as pltpu
from jax.sharding import PartitionSpec as P

NG = 80
NP = 2
PAD = 128
QUARTERS = 4
CHUNKS = 5
highest = lax.Precision.HIGHEST


def tables(length):
    indices = np.arange(length)
    nyquist = length // 2
    frequency = np.where(indices <= nyquist, indices, indices - nyquist)
    angles = 2.0 * np.pi / length * (frequency[:, None] * indices[None, :] % length)
    edges = (indices == 0) | (indices == nyquist)
    weights = np.where(edges, 1.0 / length, 2.0 / length)
    fourier = np.where((indices <= nyquist)[:, None], np.cos(angles), np.sin(angles))
    fourier = (fourier * np.sqrt(weights)[:, None]).astype(np.float32)
    squares = ((2.0 * np.pi / length * frequency) ** 2).astype(np.float32)
    return fourier, squares


def halves(table):
    high = table.astype(jnp.bfloat16)
    low = (table - high.astype(np.float32)).astype(jnp.bfloat16)
    return high, low


def left_table(table):
    high, low = halves(table)
    return np.concatenate([high, high, low], axis=1)


def right_table(table, depth):
    high, low = halves(table)
    result = np.zeros((depth, 2 * PAD), dtype=high.dtype)
    result[: table.shape[0], : table.shape[1]] = high
    result[: table.shape[0], PAD : PAD + table.shape[1]] = low
    return result


def barrier_all(me, count):
    barrier = pltpu.get_barrier_semaphore()
    for step in range(1, count):
        pl.semaphore_signal(
            barrier, inc=1, device_id={"band": lax.rem(me + step, count)},
            device_id_type=pl.DeviceIdType.MESH,
        )
    pl.semaphore_wait(barrier, count - 1)


def remote(source, target, send, receive, device):
    return pltpu.make_async_remote_copy(
        src_ref=source, dst_ref=target, send_sem=send, recv_sem=receive,
        device_id={"band": device}, device_id_type=pl.DeviceIdType.MESH,
    )


def share_kernel(count, row, partners, first_send, column_send, plane_send, receive, own_sem):
    me = lax.axis_index("band")
    planes = count // QUARTERS
    stride = count // NP
    column = lax.rem(me, QUARTERS)
    plane = lax.div(me, QUARTERS)
    base = plane * QUARTERS
    barrier_all(me, count)

    def first(r, q, c):
        return remote(row.at[q, c], partners.at[r, q, c], first_send.at[q - 1, c],
                      receive.at[r, q, c], lax.rem(me + q, count))

    def down(r, step, c):
        other = lax.rem(me + step * QUARTERS, count)
        return remote(partners.at[r, column, c], partners.at[r, column, c],
                      column_send.at[r, step - 1, c], receive.at[r, column, c], other)

    def neighbour(step):
        return base + lax.rem(column + step, QUARTERS)

    def across(r, step, c):
        return remote(partners.at[r, column, c], partners.at[r, column, c],
                      plane_send.at[r, step - 1, c], receive.at[r, column, c], neighbour(step))

    def arrived(r, q, c):
        remote(partners.at[r, q, c], partners.at[r, q, c], plane_send.at[r, 0, c],
               receive.at[r, q, c], me).wait_recv()

    for r in range(NP):
        @pl.when(me == r * stride)
        def _():
            for c in range(CHUNKS):
                for q in range(1, QUARTERS):
                    first(r, q, c).start()
            own = pltpu.make_async_copy(row, partners.at[r], own_sem)
            own.start()
            own.wait()

    for c in range(CHUNKS):
        for r in range(NP):
            @pl.when(me != r * stride)
            def _():
                arrived(r, column, c)

            @pl.when(plane == r * stride // QUARTERS)
            def _():
                for step in range(1, planes):
                    down(r, step, c).start()

            for step in range(1, QUARTERS):
                @pl.when(neighbour(step) != r * stride)
                def _():
                    across(r, step, c).start()

    for r in range(NP):
        @pl.when(me != r * stride)
        def _():
            for c in range(CHUNKS):
                for step in range(1, QUARTERS):
                    arrived(r, lax.rem(column + step, QUARTERS), c)

        @pl.when(me == r * stride)
        def _():
            for c in range(CHUNKS):
                for q in range(1, QUARTERS):
                    first(r, q, c).wait_send()

        @pl.when(plane == r * stride // QUARTERS)
        def _():
            for c in range(CHUNKS):
                for step in range(1, planes):
                    down(r, step, c).wait_send()

        for step in range(1, QUARTERS):
            @pl.when(neighbour(step) != r * stride)
            def _():
                for c in range(CHUNKS):
                    across(r, step, c).wait_send()


def share(row, count):
    planes = count // QUARTERS
    anywhere = pl.BlockSpec(memory_space=pl.ANY)
    dma = pltpu.SemaphoreType.DMA
    return pl.pallas_call(
        functools.partial(share_kernel, count),
        out_shape=jax.ShapeDtypeStruct((NP,) + row.shape, row.dtype),
        in_specs=[anywhere],
        out_specs=anywhere,
        scratch_shapes=[
            dma((QUARTERS - 1, CHUNKS)), dma((NP, planes - 1, CHUNKS)),
            dma((NP, QUARTERS - 1, CHUNKS)), dma((NP, QUARTERS, CHUNKS)), dma,
        ],
        compiler_params=pltpu.CompilerParams(
            collective_id=0, has_side_effects=True, vmem_limit_bytes=1 << 20
        ),
        name="share",
    )(row)


def sum_kernel(count, part, total, held, send, receive):
    me = lax.axis_index("band")
    barrier_all(me, count)

    def copy(step):
        return remote(part, held.at[step], send.at[step], receive.at[step],
                      lax.rem(me + step, count))

    for step in range(1, count):
        copy(step).start()
    held[0] = part[...]
    for step in range(1, count):
        copy(step).wait()
    total[...] = jnp.sum(held[...], axis=0)


def sum_all(part, count):
    rows, columns = part.shape
    width = -(-columns // PAD) * PAD
    padded = jnp.pad(part, ((0, 0), (0, width - columns)))
    vmem = pl.BlockSpec(memory_space=pltpu.VMEM)
    total = pl.pallas_call(
        functools.partial(sum_kernel, count),
        out_shape=jax.ShapeDtypeStruct((rows, width), jnp.float32),
        in_specs=[vmem],
        out_specs=vmem,
        scratch_shapes=[
            pltpu.VMEM((count, rows, width), jnp.float32),
            pltpu.SemaphoreType.DMA((count,)),
            pltpu.SemaphoreType.DMA((count,)),
        ],
        compiler_params=pltpu.CompilerParams(collective_id=1, has_side_effects=True),
        name="sum_all",
    )(padded)
    return total[:, :columns]


def pick_kernel(orbitals, first, last):
    owned, width = orbitals.shape
    values = orbitals[...].astype(jnp.float32)
    first[...] = values[0:1].reshape(width // PAD, PAD).astype(first.dtype)
    last[...] = values[owned - 1 : owned].reshape(width // PAD, PAD).astype(last.dtype)


def pick(orbitals):
    owned, points = orbitals.shape
    steps = 10
    width = points // steps
    row = jax.ShapeDtypeStruct((points // PAD, PAD), orbitals.dtype)
    spec = pl.BlockSpec((width // PAD, PAD), lambda i: (i, 0))
    return pl.pallas_call(
        pick_kernel,
        grid=(steps,),
        out_shape=(row, row),
        in_specs=[pl.BlockSpec((owned, width), lambda i: (0, i))],
        out_specs=(spec, spec),
        compiler_params=pltpu.CompilerParams(vmem_limit_bytes=32 << 20),
        name="pick",
    )(orbitals)


def split(values):
    high = values.astype(jnp.bfloat16)
    low = (values - high.astype(jnp.float32)).astype(jnp.bfloat16)
    return high, low


def dot(left, right):
    return lax.dot_general(left, right, (((1,), (0,)), ((), ())),
                           preferred_element_type=jnp.float32)


def from_left(table, values):
    high, low = split(values)
    return dot(table, jnp.concatenate([high, low, high], axis=0))


def from_right(values, table):
    high, low = split(values)
    both = dot(high, table)
    return both[:, :PAD] + both[:, PAD:] + dot(low, table[:, :PAD])


def exchange_kernel(count, target, partners, forward_left, inverse_left, forward_right,
                    inverse_right, row_squares, lane_squares, slabs, vectors, gathered, one, two,
                    send, receive, own_sem):
    group = 8
    me = lax.axis_index("band")
    barrier_all(me, count)

    def slab(step):
        other = lax.rem(me + step, count)
        return remote(slabs.at[other], gathered.at[me], send.at[step], receive.at[step], other)

    for step in range(1, count):
        slab(step).start()
    own = pltpu.make_async_copy(slabs.at[me], gathered.at[me], own_sem)
    own.start()

    def ahead(step, carry):
        planes = pl.ds(step * group, group)
        left = target[planes].astype(jnp.float32)
        parts = []
        for r in range(NP):
            density = left * partners[r, planes].astype(jnp.float32)
            parts.append(from_right(density.reshape(group * NG, NG), forward_right[...]))
        values = jnp.concatenate(parts, axis=1).reshape(group, NG, NP * PAD)
        out = jnp.stack([from_left(forward_left[...], values[i]) for i in range(group)])
        one[:, pl.ds(pl.multiple_of(step * group, group), group), :] = jnp.swapaxes(out, 0, 1)
        return carry

    lax.fori_loop(0, NG // group, ahead, 0)

    def middle(step, carry):
        outs = []
        for i in range(group):
            number = step * group + i
            folded = jnp.where(number <= NG // 2, number, number - NG // 2)
            wave = (2.0 * np.pi / NG) * folded.astype(jnp.float32)
            totals = row_squares[...] + lane_squares[...] + wave * wave
            weight = jnp.where(totals > 0.0, 1.0 / (0.0025 + totals), 0.0)
            spectrum = from_left(forward_left[...], one[number]) * weight
            outs.append(from_left(inverse_left[...], spectrum))
        out = jnp.stack(outs)
        two[:, pl.ds(pl.multiple_of(step * group, group), group), :] = jnp.swapaxes(out, 0, 1)
        return carry

    lax.fori_loop(0, NG // group, middle, 0)

    def back(step, carry):
        planes = pl.ds(step * group, group)
        values = jnp.stack(
            [from_left(inverse_left[...], two[step * group + i]) for i in range(group)]
        ).reshape(group * NG, NP * PAD)
        total = jnp.zeros((group, NG, NG), jnp.float32)
        for r in range(NP):
            potential = from_right(values[:, r * PAD : (r + 1) * PAD], inverse_right[...])
            potential = potential.reshape(group, NG, PAD)[:, :, :NG]
            total -= partners[r, planes].astype(jnp.float32) * potential
        vectors[planes] = total
        return carry

    lax.fori_loop(0, NG // group, back, 0)
    own.wait()
    for step in range(1, count):
        slab(step).wait()


def exchange(target, partners, slabs, count):
    fourier, squares = tables(NG)
    lanes = np.zeros((PAD,), np.float32)
    lanes[:NG] = squares
    vmem = pl.BlockSpec(memory_space=pltpu.VMEM)
    anywhere = pl.BlockSpec(memory_space=pl.ANY)
    dma = pltpu.SemaphoreType.DMA
    return pl.pallas_call(
        functools.partial(exchange_kernel, count),
        out_shape=(
            jax.ShapeDtypeStruct((NG, NG, NG), jnp.float32),
            jax.ShapeDtypeStruct(slabs.shape, slabs.dtype),
        ),
        in_specs=[vmem] * 8 + [anywhere],
        out_specs=(vmem, anywhere),
        scratch_shapes=[pltpu.VMEM((NG, NG, NP * PAD), jnp.float32)] * 2
        + [dma((count,)), dma((count,)), dma],
        compiler_params=pltpu.CompilerParams(
            collective_id=2, has_side_effects=True, vmem_limit_bytes=48 << 20
        ),
        cost_estimate=pl.CostEstimate(
            flops=12 * NP * NG**4, bytes_accessed=8 << 20, transcendentals=0
        ),
        name="exchange",
    )(
        target,
        partners,
        left_table(fourier),
        left_table(fourier.T.copy()),
        right_table(fourier.T.copy(), NG),
        right_table(fourier, PAD),
        np.broadcast_to(squares[:, None], (NG, NP * PAD)).copy(),
        np.tile(lanes, NP)[None, :],
        slabs,
    )


def body(orbitals):
    devices = lax.axis_size("band")
    points = orbitals.shape[1]
    target, row = pick(orbitals)
    partners = share(row.reshape(QUARTERS, CHUNKS, -1, PAD), devices)
    vectors, target_slab = exchange(
        target.reshape(NG, NG, NG),
        partners.reshape(NP, NG, NG, NG),
        target.reshape(devices, 8, points // devices // 8),
        devices,
    )
    vector_slab = lax.all_to_all(
        vectors.reshape(1, points), "band", split_axis=1, concat_axis=0, tiled=True
    )
    target_slab = target_slab.reshape(devices, points // devices).astype(jnp.float32)
    part = jnp.einsum("ap,bp->ab", target_slab, vector_slab, precision=highest) / NG**3
    intersection = sum_all(part, devices)
    metric = -0.5 * (intersection + intersection.T)
    factor = jnp.linalg.cholesky(metric)
    return jax.scipy.linalg.solve_triangular(factor, vector_slab, lower=True)


def solution(mesh):
    placed = (P(("spin", "band"), None),)
    return jax.shard_map(
        body, mesh=mesh, in_specs=placed, out_specs=P("spin", "band"), check_vma=False
    )
```

```python
import functools

import jax
import jax.numpy as jnp
import numpy as np
from jax import lax
from jax.experimental import pallas as pl
from jax.experimental.pallas import tpu as pltpu
from jax.sharding import PartitionSpec as P

NG = 80
NP = 2
PAD = 128
QUARTERS = 4
CHUNKS = 5
highest = lax.Precision.HIGHEST


def tables(length):
    indices = np.arange(length)
    nyquist = length // 2
    frequency = np.where(indices <= nyquist, indices, indices - nyquist)
    angles = 2.0 * np.pi / length * (frequency[:, None] * indices[None, :] % length)
    edges = (indices == 0) | (indices == nyquist)
    weights = np.where(edges, 1.0 / length, 2.0 / length)
    fourier = np.where((indices <= nyquist)[:, None], np.cos(angles), np.sin(angles))
    fourier = (fourier * np.sqrt(weights)[:, None]).astype(np.float32)
    squares = ((2.0 * np.pi / length * frequency) ** 2).astype(np.float32)
    return fourier, squares


def halves(table):
    high = table.astype(jnp.bfloat16)
    low = (table - high.astype(np.float32)).astype(jnp.bfloat16)
    return high, low


def left_table(table):
    high, low = halves(table)
    return np.concatenate([high, high, low], axis=1)


def right_table(table, depth):
    high, low = halves(table)
    result = np.zeros((depth, 2 * PAD), dtype=high.dtype)
    result[: table.shape[0], : table.shape[1]] = high
    result[: table.shape[0], PAD : PAD + table.shape[1]] = low
    return result


def barrier_all(me, count):
    barrier = pltpu.get_barrier_semaphore()
    for step in range(1, count):
        pl.semaphore_signal(
            barrier, inc=1, device_id={"band": lax.rem(me + step, count)},
            device_id_type=pl.DeviceIdType.MESH,
        )
    pl.semaphore_wait(barrier, count - 1)


def remote(source, target, send, receive, device):
    return pltpu.make_async_remote_copy(
        src_ref=source, dst_ref=target, send_sem=send, recv_sem=receive,
        device_id={"band": device}, device_id_type=pl.DeviceIdType.MESH,
    )


def share_kernel(count, row, partners, first_send, column_send, plane_send, receive, own_sem):
    me = lax.axis_index("band")
    planes = count // QUARTERS
    stride = count // NP
    column = lax.rem(me, QUARTERS)
    plane = lax.div(me, QUARTERS)
    base = plane * QUARTERS
    barrier_all(me, count)

    def first(r, q, c):
        return remote(row.at[q, c], partners.at[r, q, c], first_send.at[q - 1, c],
                      receive.at[r, q, c], lax.rem(me + q, count))

    def down(r, step, c):
        other = lax.rem(me + step * QUARTERS, count)
        return remote(partners.at[r, column, c], partners.at[r, column, c],
                      column_send.at[r, step - 1, c], receive.at[r, column, c], other)

    def neighbour(step):
        return base + lax.rem(column + step, QUARTERS)

    def across(r, step, c):
        return remote(partners.at[r, column, c], partners.at[r, column, c],
                      plane_send.at[r, step - 1, c], receive.at[r, column, c], neighbour(step))

    def arrived(r, q, c):
        remote(partners.at[r, q, c], partners.at[r, q, c], plane_send.at[r, 0, c],
               receive.at[r, q, c], me).wait_recv()

    for r in range(NP):
        @pl.when(me == r * stride)
        def _():
            for c in range(CHUNKS):
                for q in range(1, QUARTERS):
                    first(r, q, c).start()
            own = pltpu.make_async_copy(row, partners.at[r], own_sem)
            own.start()
            own.wait()

    for c in range(CHUNKS):
        for r in range(NP):
            @pl.when(me != r * stride)
            def _():
                arrived(r, column, c)

            @pl.when(plane == r * stride // QUARTERS)
            def _():
                for step in range(1, planes):
                    down(r, step, c).start()

            for step in range(1, QUARTERS):
                @pl.when(neighbour(step) != r * stride)
                def _():
                    across(r, step, c).start()

    for r in range(NP):
        @pl.when(me != r * stride)
        def _():
            for c in range(CHUNKS):
                for step in range(1, QUARTERS):
                    arrived(r, lax.rem(column + step, QUARTERS), c)

        @pl.when(me == r * stride)
        def _():
            for c in range(CHUNKS):
                for q in range(1, QUARTERS):
                    first(r, q, c).wait_send()

        @pl.when(plane == r * stride // QUARTERS)
        def _():
            for c in range(CHUNKS):
                for step in range(1, planes):
                    down(r, step, c).wait_send()

        for step in range(1, QUARTERS):
            @pl.when(neighbour(step) != r * stride)
            def _():
                for c in range(CHUNKS):
                    across(r, step, c).wait_send()


def share(row, count):
    planes = count // QUARTERS
    anywhere = pl.BlockSpec(memory_space=pl.ANY)
    dma = pltpu.SemaphoreType.DMA
    return pl.pallas_call(
        functools.partial(share_kernel, count),
        out_shape=jax.ShapeDtypeStruct((NP,) + row.shape, row.dtype),
        in_specs=[anywhere],
        out_specs=anywhere,
        scratch_shapes=[
            dma((QUARTERS - 1, CHUNKS)), dma((NP, planes - 1, CHUNKS)),
            dma((NP, QUARTERS - 1, CHUNKS)), dma((NP, QUARTERS, CHUNKS)), dma,
        ],
        compiler_params=pltpu.CompilerParams(
            collective_id=0, has_side_effects=True, vmem_limit_bytes=1 << 20
        ),
        name="share",
    )(row)


def sum_kernel(count, part, total, held, send, receive):
    me = lax.axis_index("band")
    barrier_all(me, count)

    def copy(step):
        return remote(part, held.at[step], send.at[step], receive.at[step],
                      lax.rem(me + step, count))

    for step in range(1, count):
        copy(step).start()
    held[0] = part[...]
    for step in range(1, count):
        copy(step).wait()
    total[...] = jnp.sum(held[...], axis=0)


def sum_all(part, count):
    vmem = pl.BlockSpec(memory_space=pltpu.VMEM)
    return pl.pallas_call(
        functools.partial(sum_kernel, count),
        out_shape=jax.ShapeDtypeStruct(part.shape, jnp.float32),
        in_specs=[vmem],
        out_specs=vmem,
        scratch_shapes=[
            pltpu.VMEM((count,) + part.shape, jnp.float32),
            pltpu.SemaphoreType.DMA((count,)),
            pltpu.SemaphoreType.DMA((count,)),
        ],
        compiler_params=pltpu.CompilerParams(
            collective_id=1, has_side_effects=True, vmem_limit_bytes=4 << 20
        ),
        name="sum_all",
    )(part)


def pick_kernel(orbitals, first, last):
    owned, width = orbitals.shape
    values = orbitals[...].astype(jnp.float32)
    first[...] = values[0:1].reshape(width // PAD, PAD).astype(first.dtype)
    last[...] = values[owned - 1 : owned].reshape(width // PAD, PAD).astype(last.dtype)


def pick(orbitals):
    owned, points = orbitals.shape
    steps = 10
    width = points // steps
    row = jax.ShapeDtypeStruct((points // PAD, PAD), orbitals.dtype)
    spec = pl.BlockSpec((width // PAD, PAD), lambda i: (i, 0))
    return pl.pallas_call(
        pick_kernel,
        grid=(steps,),
        out_shape=(row, row),
        in_specs=[pl.BlockSpec((owned, width), lambda i: (0, i))],
        out_specs=(spec, spec),
        compiler_params=pltpu.CompilerParams(vmem_limit_bytes=6 << 20),
        name="pick",
    )(orbitals)


def split(values):
    high = values.astype(jnp.bfloat16)
    low = (values - high.astype(jnp.float32)).astype(jnp.bfloat16)
    return high, low


def dot(left, right):
    return lax.dot_general(left, right, (((1,), (0,)), ((), ())),
                           preferred_element_type=jnp.float32)


def from_left(table, values):
    high, low = split(values)
    return dot(table, jnp.concatenate([high, low, high], axis=0))


def from_right(values, table):
    high, low = split(values)
    both = dot(high, table)
    return both[:, :PAD] + both[:, PAD:] + dot(low, table[:, :PAD])


def exchange_kernel(count, target, partners, forward_left, inverse_left, forward_right,
                    inverse_right, row_squares, lane_squares, slabs, vectors, gathered, one, two,
                    send, receive, own_sem):
    group = 8
    me = lax.axis_index("band")
    barrier_all(me, count)

    def slab(step):
        other = lax.rem(me + step, count)
        return remote(slabs.at[other], gathered.at[me], send.at[step], receive.at[step], other)

    for step in range(1, count):
        slab(step).start()
    own = pltpu.make_async_copy(slabs.at[me], gathered.at[me], own_sem)
    own.start()

    def ahead(step, carry):
        planes = pl.ds(step * group, group)
        left = target[planes].astype(jnp.float32)
        parts = []
        for r in range(NP):
            density = left * partners[r, planes].astype(jnp.float32)
            parts.append(from_right(density.reshape(group * NG, NG), forward_right[...]))
        values = jnp.concatenate(parts, axis=1).reshape(group, NG, NP * PAD)
        out = jnp.stack([from_left(forward_left[...], values[i]) for i in range(group)])
        one[:, pl.ds(pl.multiple_of(step * group, group), group), :] = jnp.swapaxes(out, 0, 1)
        return carry

    lax.fori_loop(0, NG // group, ahead, 0)

    def middle(step, carry):
        outs = []
        for i in range(group):
            number = step * group + i
            folded = jnp.where(number <= NG // 2, number, number - NG // 2)
            wave = (2.0 * np.pi / NG) * folded.astype(jnp.float32)
            totals = row_squares[...] + lane_squares[...] + wave * wave
            weight = jnp.where(totals > 0.0, 1.0 / (0.0025 + totals), 0.0)
            spectrum = from_left(forward_left[...], one[number]) * weight
            outs.append(from_left(inverse_left[...], spectrum))
        out = jnp.stack(outs)
        two[:, pl.ds(pl.multiple_of(step * group, group), group), :] = jnp.swapaxes(out, 0, 1)
        return carry

    lax.fori_loop(0, NG // group, middle, 0)

    def back(step, carry):
        planes = pl.ds(step * group, group)
        values = jnp.stack(
            [from_left(inverse_left[...], two[step * group + i]) for i in range(group)]
        ).reshape(group * NG, NP * PAD)
        total = jnp.zeros((group, NG, NG), jnp.float32)
        for r in range(NP):
            potential = from_right(values[:, r * PAD : (r + 1) * PAD], inverse_right[...])
            potential = potential.reshape(group, NG, PAD)[:, :, :NG]
            total -= partners[r, planes].astype(jnp.float32) * potential
        vectors[planes] = total
        return carry

    lax.fori_loop(0, NG // group, back, 0)
    own.wait()
    for step in range(1, count):
        slab(step).wait()


def exchange(target, partners, slabs, count):
    fourier, squares = tables(NG)
    lanes = np.zeros((PAD,), np.float32)
    lanes[:NG] = squares
    vmem = pl.BlockSpec(memory_space=pltpu.VMEM)
    anywhere = pl.BlockSpec(memory_space=pl.ANY)
    dma = pltpu.SemaphoreType.DMA
    return pl.pallas_call(
        functools.partial(exchange_kernel, count),
        out_shape=(
            jax.ShapeDtypeStruct((NG, NG, NG), jnp.float32),
            jax.ShapeDtypeStruct(slabs.shape, slabs.dtype),
        ),
        in_specs=[vmem] * 8 + [anywhere],
        out_specs=(vmem, anywhere),
        scratch_shapes=[pltpu.VMEM((NG, NG, NP * PAD), jnp.float32)] * 2
        + [dma((count,)), dma((count,)), dma],
        compiler_params=pltpu.CompilerParams(
            collective_id=2, has_side_effects=True, vmem_limit_bytes=48 << 20
        ),
        cost_estimate=pl.CostEstimate(
            flops=12 * NP * NG**4, bytes_accessed=8 << 20, transcendentals=0
        ),
        name="exchange",
    )(
        target,
        partners,
        left_table(fourier),
        left_table(fourier.T.copy()),
        right_table(fourier.T.copy(), NG),
        right_table(fourier, PAD),
        np.broadcast_to(squares[:, None], (NG, NP * PAD)).copy(),
        np.tile(lanes, NP)[None, :],
        slabs,
    )


def body(orbitals):
    devices = lax.axis_size("band")
    points = orbitals.shape[1]
    target, row = pick(orbitals)
    partners = share(row.reshape(QUARTERS, CHUNKS, -1, PAD), devices)
    vectors, target_slab = exchange(
        target.reshape(NG, NG, NG),
        partners.reshape(NP, NG, NG, NG),
        target.reshape(devices, 8, points // devices // 8),
        devices,
    )
    vector_slab = lax.all_to_all(
        vectors.reshape(1, points), "band", split_axis=1, concat_axis=0, tiled=True
    )
    target_slab = target_slab.reshape(devices, points // devices).astype(jnp.float32)
    part = jnp.einsum("ap,bp->ab", target_slab, vector_slab, precision=highest) / NG**3
    intersection = sum_all(part, devices)
    metric = -0.5 * (intersection + intersection.T)
    factor = lax.linalg.cholesky(metric, symmetrize_input=False)
    return jax.scipy.linalg.solve_triangular(factor, vector_slab, lower=True)


def solution(mesh):
    placed = (P(("spin", "band"), None),)
    return jax.shard_map(
        body, mesh=mesh, in_specs=placed, out_specs=P("spin", "band"), check_vma=False
    )
```

```python
import functools

import jax
import jax.numpy as jnp
import numpy as np
from jax import lax
from jax.experimental import pallas as pl
from jax.experimental.pallas import tpu as pltpu
from jax.sharding import PartitionSpec as P

NG = 80
NP = 2
PAD = 128
QUARTERS = 4
CHUNKS = 5
highest = lax.Precision.HIGHEST


def tables(length):
    indices = np.arange(length)
    nyquist = length // 2
    frequency = np.where(indices <= nyquist, indices, indices - nyquist)
    angles = 2.0 * np.pi / length * (frequency[:, None] * indices[None, :] % length)
    edges = (indices == 0) | (indices == nyquist)
    weights = np.where(edges, 1.0 / length, 2.0 / length)
    fourier = np.where((indices <= nyquist)[:, None], np.cos(angles), np.sin(angles))
    fourier = (fourier * np.sqrt(weights)[:, None]).astype(np.float32)
    squares = ((2.0 * np.pi / length * frequency) ** 2).astype(np.float32)
    return fourier, squares


def halves(table):
    high = table.astype(jnp.bfloat16)
    low = (table - high.astype(np.float32)).astype(jnp.bfloat16)
    return high, low


def left_table(table):
    high, low = halves(table)
    return np.concatenate([high, high, low], axis=1)


def right_table(table, depth):
    high, low = halves(table)
    result = np.zeros((depth, 2 * PAD), dtype=high.dtype)
    result[: table.shape[0], : table.shape[1]] = high
    result[: table.shape[0], PAD : PAD + table.shape[1]] = low
    return result


def barrier_all(me, count):
    barrier = pltpu.get_barrier_semaphore()
    for step in range(1, count):
        pl.semaphore_signal(
            barrier, inc=1, device_id={"band": lax.rem(me + step, count)},
            device_id_type=pl.DeviceIdType.MESH,
        )
    pl.semaphore_wait(barrier, count - 1)


def remote(source, target, send, receive, device):
    return pltpu.make_async_remote_copy(
        src_ref=source, dst_ref=target, send_sem=send, recv_sem=receive,
        device_id={"band": device}, device_id_type=pl.DeviceIdType.MESH,
    )


def share_kernel(count, row, partners, first_send, column_send, plane_send, receive, own_sem):
    me = lax.axis_index("band")
    planes = count // QUARTERS
    stride = count // NP
    column = lax.rem(me, QUARTERS)
    plane = lax.div(me, QUARTERS)
    base = plane * QUARTERS
    barrier_all(me, count)

    def first(r, q, c):
        return remote(row.at[q, c], partners.at[r, q, c], first_send.at[q - 1, c],
                      receive.at[r, q, c], lax.rem(me + q, count))

    def down(r, step, c):
        other = lax.rem(me + step * QUARTERS, count)
        return remote(partners.at[r, column, c], partners.at[r, column, c],
                      column_send.at[r, step - 1, c], receive.at[r, column, c], other)

    def neighbour(step):
        return base + lax.rem(column + step, QUARTERS)

    def across(r, step, c):
        return remote(partners.at[r, column, c], partners.at[r, column, c],
                      plane_send.at[r, step - 1, c], receive.at[r, column, c], neighbour(step))

    def arrived(r, q, c):
        remote(partners.at[r, q, c], partners.at[r, q, c], plane_send.at[r, 0, c],
               receive.at[r, q, c], me).wait_recv()

    for r in range(NP):
        @pl.when(me == r * stride)
        def _():
            for c in range(CHUNKS):
                for q in range(1, QUARTERS):
                    first(r, q, c).start()
            own = pltpu.make_async_copy(row, partners.at[r], own_sem)
            own.start()
            own.wait()

    for c in range(CHUNKS):
        for r in range(NP):
            @pl.when(me != r * stride)
            def _():
                arrived(r, column, c)

            @pl.when(plane == r * stride // QUARTERS)
            def _():
                for step in range(1, planes):
                    down(r, step, c).start()

            for step in range(1, QUARTERS):
                @pl.when(neighbour(step) != r * stride)
                def _():
                    across(r, step, c).start()

    for r in range(NP):
        @pl.when(me != r * stride)
        def _():
            for c in range(CHUNKS):
                for step in range(1, QUARTERS):
                    arrived(r, lax.rem(column + step, QUARTERS), c)

        @pl.when(me == r * stride)
        def _():
            for c in range(CHUNKS):
                for q in range(1, QUARTERS):
                    first(r, q, c).wait_send()

        @pl.when(plane == r * stride // QUARTERS)
        def _():
            for c in range(CHUNKS):
                for step in range(1, planes):
                    down(r, step, c).wait_send()

        for step in range(1, QUARTERS):
            @pl.when(neighbour(step) != r * stride)
            def _():
                for c in range(CHUNKS):
                    across(r, step, c).wait_send()


def share(row, count):
    planes = count // QUARTERS
    anywhere = pl.BlockSpec(memory_space=pl.ANY)
    dma = pltpu.SemaphoreType.DMA
    return pl.pallas_call(
        functools.partial(share_kernel, count),
        out_shape=jax.ShapeDtypeStruct((NP,) + row.shape, row.dtype),
        in_specs=[pl.BlockSpec(memory_space=pltpu.HBM)],
        out_specs=anywhere,
        scratch_shapes=[
            dma((QUARTERS - 1, CHUNKS)), dma((NP, planes - 1, CHUNKS)),
            dma((NP, QUARTERS - 1, CHUNKS)), dma((NP, QUARTERS, CHUNKS)), dma,
        ],
        compiler_params=pltpu.CompilerParams(
            collective_id=0, has_side_effects=True, vmem_limit_bytes=60 << 20
        ),
        name="share",
    )(row)


def sum_kernel(count, part, total, held, send, receive):
    me = lax.axis_index("band")
    barrier_all(me, count)

    def copy(step):
        return remote(part, held.at[step], send.at[step], receive.at[step],
                      lax.rem(me + step, count))

    for step in range(1, count):
        copy(step).start()
    held[0] = part[...]
    for step in range(1, count):
        copy(step).wait()
    total[...] = jnp.sum(held[...], axis=0)


def sum_all(part, count):
    vmem = pl.BlockSpec(memory_space=pltpu.VMEM)
    return pl.pallas_call(
        functools.partial(sum_kernel, count),
        out_shape=jax.ShapeDtypeStruct(part.shape, jnp.float32),
        in_specs=[vmem],
        out_specs=vmem,
        scratch_shapes=[
            pltpu.VMEM((count,) + part.shape, jnp.float32),
            pltpu.SemaphoreType.DMA((count,)),
            pltpu.SemaphoreType.DMA((count,)),
        ],
        compiler_params=pltpu.CompilerParams(
            collective_id=1, has_side_effects=True, vmem_limit_bytes=4 << 20
        ),
        name="sum_all",
    )(part)


def pick_kernel(orbitals, first, last):
    owned, width = orbitals.shape
    values = orbitals[...].astype(jnp.float32)
    first[...] = values[0:1].reshape(width // PAD, PAD).astype(first.dtype)
    last[...] = values[owned - 1 : owned].reshape(width // PAD, PAD).astype(last.dtype)


def pick(orbitals):
    owned, points = orbitals.shape
    steps = 10
    width = points // steps
    row = jax.ShapeDtypeStruct((points // PAD, PAD), orbitals.dtype)
    spec = pl.BlockSpec((width // PAD, PAD), lambda i: (i, 0))
    return pl.pallas_call(
        pick_kernel,
        grid=(steps,),
        out_shape=(row, row),
        in_specs=[pl.BlockSpec((owned, width), lambda i: (0, i))],
        out_specs=(spec, spec),
        compiler_params=pltpu.CompilerParams(vmem_limit_bytes=6 << 20),
        name="pick",
    )(orbitals)


def split(values):
    high = values.astype(jnp.bfloat16)
    low = (values - high.astype(jnp.float32)).astype(jnp.bfloat16)
    return high, low


def dot(left, right):
    return lax.dot_general(left, right, (((1,), (0,)), ((), ())),
                           preferred_element_type=jnp.float32)


def from_left(table, values):
    high, low = split(values)
    return dot(table, jnp.concatenate([high, low, high], axis=0))


def from_right(values, table):
    high, low = split(values)
    both = dot(high, table)
    return both[:, :PAD] + both[:, PAD:] + dot(low, table[:, :PAD])


def exchange_kernel(count, target_in, partners_in, forward_left, inverse_left, forward_right,
                    inverse_right, row_squares, lane_squares, slabs, vectors, gathered, one, two,
                    target, partners, done, send, receive, own_sem, load_sem, done_sem):
    group = 8
    me = lax.axis_index("band")
    loads = [
        pltpu.make_async_copy(target_in, target, load_sem.at[0]),
        pltpu.make_async_copy(partners_in, partners, load_sem.at[1]),
    ]
    for load in loads:
        load.start()
    barrier_all(me, count)

    def slab(step):
        other = lax.rem(me + step, count)
        return remote(slabs.at[other], gathered.at[me], send.at[step], receive.at[step], other)

    for step in range(1, count):
        slab(step).start()
    own = pltpu.make_async_copy(slabs.at[me], gathered.at[me], own_sem)
    own.start()
    for load in loads:
        load.wait()

    def ahead(step, carry):
        planes = pl.ds(step * group, group)
        left = target[planes].astype(jnp.float32)
        parts = []
        for r in range(NP):
            density = left * partners[r, planes].astype(jnp.float32)
            parts.append(from_right(density.reshape(group * NG, NG), forward_right[...]))
        values = jnp.concatenate(parts, axis=1).reshape(group, NG, NP * PAD)
        out = jnp.stack([from_left(forward_left[...], values[i]) for i in range(group)])
        one[:, pl.ds(pl.multiple_of(step * group, group), group), :] = jnp.swapaxes(out, 0, 1)
        return carry

    lax.fori_loop(0, NG // group, ahead, 0)

    def middle(step, carry):
        outs = []
        for i in range(group):
            number = step * group + i
            folded = jnp.where(number <= NG // 2, number, number - NG // 2)
            wave = (2.0 * np.pi / NG) * folded.astype(jnp.float32)
            totals = row_squares[...] + lane_squares[...] + wave * wave
            weight = jnp.where(totals > 0.0, 1.0 / (0.0025 + totals), 0.0)
            spectrum = from_left(forward_left[...], one[number]) * weight
            outs.append(from_left(inverse_left[...], spectrum))
        out = jnp.stack(outs)
        two[:, pl.ds(pl.multiple_of(step * group, group), group), :] = jnp.swapaxes(out, 0, 1)
        return carry

    lax.fori_loop(0, NG // group, middle, 0)

    def back(step, carry):
        planes = pl.ds(step * group, group)
        values = jnp.stack(
            [from_left(inverse_left[...], two[step * group + i]) for i in range(group)]
        ).reshape(group * NG, NP * PAD)
        total = jnp.zeros((group, NG, NG), jnp.float32)
        for r in range(NP):
            potential = from_right(values[:, r * PAD : (r + 1) * PAD], inverse_right[...])
            potential = potential.reshape(group, NG, PAD)[:, :, :NG]
            total -= partners[r, planes].astype(jnp.float32) * potential
        done[planes] = total
        stored(step).start()
        return carry

    def stored(step):
        planes = pl.ds(step * group, group)
        return pltpu.make_async_copy(done.at[planes], vectors.at[planes], done_sem.at[step])

    lax.fori_loop(0, NG // group, back, 0)
    for step in range(NG // group):
        stored(step).wait()
    own.wait()
    for step in range(1, count):
        slab(step).wait()


def exchange(target, partners, slabs, count):
    fourier, squares = tables(NG)
    lanes = np.zeros((PAD,), np.float32)
    lanes[:NG] = squares
    vmem = pl.BlockSpec(memory_space=pltpu.VMEM)
    anywhere = pl.BlockSpec(memory_space=pl.ANY)
    dma = pltpu.SemaphoreType.DMA
    return pl.pallas_call(
        functools.partial(exchange_kernel, count),
        out_shape=(
            jax.ShapeDtypeStruct((NG, NG, NG), jnp.float32),
            jax.ShapeDtypeStruct(slabs.shape, slabs.dtype),
        ),
        in_specs=[anywhere] * 2 + [vmem] * 6 + [anywhere],
        out_specs=(anywhere, anywhere),
        scratch_shapes=[pltpu.VMEM((NG, NG, NP * PAD), jnp.float32)] * 2
        + [
            pltpu.VMEM(target.shape, target.dtype),
            pltpu.VMEM(partners.shape, partners.dtype),
            pltpu.VMEM((NG, NG, NG), jnp.float32),
            dma((count,)), dma((count,)), dma, dma((2,)), dma((NG // 8,)),
        ],
        compiler_params=pltpu.CompilerParams(
            collective_id=2, has_side_effects=True, vmem_limit_bytes=60 << 20
        ),
        cost_estimate=pl.CostEstimate(
            flops=12 * NP * NG**4, bytes_accessed=8 << 20, transcendentals=0
        ),
        name="exchange",
    )(
        target,
        partners,
        left_table(fourier),
        left_table(fourier.T.copy()),
        right_table(fourier.T.copy(), NG),
        right_table(fourier, PAD),
        np.broadcast_to(squares[:, None], (NG, NP * PAD)).copy(),
        np.tile(lanes, NP)[None, :],
        slabs,
    )


def body(orbitals):
    devices = lax.axis_size("band")
    points = orbitals.shape[1]
    target, row = pick(orbitals)
    partners = share(row.reshape(QUARTERS, CHUNKS, -1, PAD), devices)
    vectors, target_slab = exchange(
        target.reshape(NG, NG, NG),
        partners.reshape(NP, NG, NG, NG),
        target.reshape(devices, 8, points // devices // 8),
        devices,
    )
    vector_slab = lax.all_to_all(
        vectors.reshape(1, points), "band", split_axis=1, concat_axis=0, tiled=True
    )
    target_slab = target_slab.reshape(devices, points // devices).astype(jnp.float32)
    part = jnp.einsum("ap,bp->ab", target_slab, vector_slab, precision=highest) / NG**3
    intersection = sum_all(part, devices)
    metric = -0.5 * (intersection + intersection.T)
    factor = lax.linalg.cholesky(metric, symmetrize_input=False)
    return jax.scipy.linalg.solve_triangular(factor, vector_slab, lower=True)


def solution(mesh):
    placed = (P(("spin", "band"), None),)
    return jax.shard_map(
        body, mesh=mesh, in_specs=placed, out_specs=P("spin", "band"), check_vma=False
    )
```

```python
import functools

import jax
import jax.numpy as jnp
import numpy as np
from jax import lax
from jax.experimental import pallas as pl
from jax.experimental.pallas import tpu as pltpu
from jax.sharding import PartitionSpec as P

NG = 80
NP = 2
PAD = 128
QUARTERS = 4
CHUNKS = 5
highest = lax.Precision.HIGHEST


def tables(length):
    indices = np.arange(length)
    nyquist = length // 2
    frequency = np.where(indices <= nyquist, indices, indices - nyquist)
    angles = 2.0 * np.pi / length * (frequency[:, None] * indices[None, :] % length)
    edges = (indices == 0) | (indices == nyquist)
    weights = np.where(edges, 1.0 / length, 2.0 / length)
    fourier = np.where((indices <= nyquist)[:, None], np.cos(angles), np.sin(angles))
    fourier = (fourier * np.sqrt(weights)[:, None]).astype(np.float32)
    squares = ((2.0 * np.pi / length * frequency) ** 2).astype(np.float32)
    return fourier, squares


def halves(table):
    high = table.astype(jnp.bfloat16)
    low = (table - high.astype(np.float32)).astype(jnp.bfloat16)
    return high, low


def left_table(table):
    high, low = halves(table)
    return np.concatenate([high, high, low], axis=1)


def right_table(table, depth):
    high, low = halves(table)
    result = np.zeros((depth, 2 * PAD), dtype=high.dtype)
    result[: table.shape[0], : table.shape[1]] = high
    result[: table.shape[0], PAD : PAD + table.shape[1]] = low
    return result


def barrier_all(me, count):
    barrier = pltpu.get_barrier_semaphore()
    for step in range(1, count):
        pl.semaphore_signal(
            barrier, inc=1, device_id={"band": lax.rem(me + step, count)},
            device_id_type=pl.DeviceIdType.MESH,
        )
    pl.semaphore_wait(barrier, count - 1)


def remote(source, target, send, receive, device):
    return pltpu.make_async_remote_copy(
        src_ref=source, dst_ref=target, send_sem=send, recv_sem=receive,
        device_id={"band": device}, device_id_type=pl.DeviceIdType.MESH,
    )


def share_kernel(count, row, partners, first_send, column_send, plane_send, receive, own_sem):
    me = lax.axis_index("band")
    planes = count // QUARTERS
    stride = count // NP
    column = lax.rem(me, QUARTERS)
    plane = lax.div(me, QUARTERS)
    base = plane * QUARTERS
    barrier_all(me, count)

    def first(r, q, c):
        return remote(row.at[q, c], partners.at[r, q, c], first_send.at[q - 1, c],
                      receive.at[r, q, c], lax.rem(me + q, count))

    def down(r, step, c):
        other = lax.rem(me + step * QUARTERS, count)
        return remote(partners.at[r, column, c], partners.at[r, column, c],
                      column_send.at[r, step - 1, c], receive.at[r, column, c], other)

    def neighbour(step):
        return base + lax.rem(column + step, QUARTERS)

    def across(r, step, c):
        return remote(partners.at[r, column, c], partners.at[r, column, c],
                      plane_send.at[r, step - 1, c], receive.at[r, column, c], neighbour(step))

    def arrived(r, q, c):
        remote(partners.at[r, q, c], partners.at[r, q, c], plane_send.at[r, 0, c],
               receive.at[r, q, c], me).wait_recv()

    for r in range(NP):
        @pl.when(me == r * stride)
        def _():
            for c in range(CHUNKS):
                for q in range(1, QUARTERS):
                    first(r, q, c).start()
            own = pltpu.make_async_copy(row, partners.at[r], own_sem)
            own.start()
            own.wait()

    for c in range(CHUNKS):
        for r in range(NP):
            @pl.when(me != r * stride)
            def _():
                arrived(r, column, c)

            @pl.when(plane == r * stride // QUARTERS)
            def _():
                for step in range(1, planes):
                    down(r, step, c).start()

            for step in range(1, QUARTERS):
                @pl.when(neighbour(step) != r * stride)
                def _():
                    across(r, step, c).start()

    for r in range(NP):
        @pl.when(me != r * stride)
        def _():
            for c in range(CHUNKS):
                for step in range(1, QUARTERS):
                    arrived(r, lax.rem(column + step, QUARTERS), c)

        @pl.when(me == r * stride)
        def _():
            for c in range(CHUNKS):
                for q in range(1, QUARTERS):
                    first(r, q, c).wait_send()

        @pl.when(plane == r * stride // QUARTERS)
        def _():
            for c in range(CHUNKS):
                for step in range(1, planes):
                    down(r, step, c).wait_send()

        for step in range(1, QUARTERS):
            @pl.when(neighbour(step) != r * stride)
            def _():
                for c in range(CHUNKS):
                    across(r, step, c).wait_send()


def share(row, count):
    planes = count // QUARTERS
    anywhere = pl.BlockSpec(memory_space=pl.ANY)
    dma = pltpu.SemaphoreType.DMA
    return pl.pallas_call(
        functools.partial(share_kernel, count),
        out_shape=jax.ShapeDtypeStruct((NP,) + row.shape, row.dtype),
        in_specs=[pl.BlockSpec(memory_space=pltpu.HBM)],
        out_specs=anywhere,
        scratch_shapes=[
            dma((QUARTERS - 1, CHUNKS)), dma((NP, planes - 1, CHUNKS)),
            dma((NP, QUARTERS - 1, CHUNKS)), dma((NP, QUARTERS, CHUNKS)), dma,
        ],
        compiler_params=pltpu.CompilerParams(
            collective_id=0, has_side_effects=True, vmem_limit_bytes=1 << 20
        ),
        name="share",
    )(row)


def sum_kernel(count, part, total, held, send, receive):
    me = lax.axis_index("band")
    barrier_all(me, count)

    def copy(step):
        return remote(part, held.at[step], send.at[step], receive.at[step],
                      lax.rem(me + step, count))

    for step in range(1, count):
        copy(step).start()
    held[0] = part[...]
    for step in range(1, count):
        copy(step).wait()
    total[...] = jnp.sum(held[...], axis=0)


def sum_all(part, count):
    vmem = pl.BlockSpec(memory_space=pltpu.VMEM)
    return pl.pallas_call(
        functools.partial(sum_kernel, count),
        out_shape=jax.ShapeDtypeStruct(part.shape, jnp.float32),
        in_specs=[vmem],
        out_specs=vmem,
        scratch_shapes=[
            pltpu.VMEM((count,) + part.shape, jnp.float32),
            pltpu.SemaphoreType.DMA((count,)),
            pltpu.SemaphoreType.DMA((count,)),
        ],
        compiler_params=pltpu.CompilerParams(
            collective_id=1, has_side_effects=True, vmem_limit_bytes=4 << 20
        ),
        name="sum_all",
    )(part)


def pick_kernel(orbitals, first, last):
    owned, width = orbitals.shape
    values = orbitals[...].astype(jnp.float32)
    first[...] = values[0:1].reshape(width // PAD, PAD).astype(first.dtype)
    last[...] = values[owned - 1 : owned].reshape(width // PAD, PAD).astype(last.dtype)


def pick(orbitals):
    owned, points = orbitals.shape
    steps = 10
    width = points // steps
    row = jax.ShapeDtypeStruct((points // PAD, PAD), orbitals.dtype)
    spec = pl.BlockSpec((width // PAD, PAD), lambda i: (i, 0))
    return pl.pallas_call(
        pick_kernel,
        grid=(steps,),
        out_shape=(row, row),
        in_specs=[pl.BlockSpec((owned, width), lambda i: (0, i))],
        out_specs=(spec, spec),
        compiler_params=pltpu.CompilerParams(vmem_limit_bytes=6 << 20),
        name="pick",
    )(orbitals)


def split(values):
    high = values.astype(jnp.bfloat16)
    low = (values - high.astype(jnp.float32)).astype(jnp.bfloat16)
    return high, low


def dot(left, right):
    return lax.dot_general(left, right, (((1,), (0,)), ((), ())),
                           preferred_element_type=jnp.float32)


def from_left(table, values):
    high, low = split(values)
    return dot(table, jnp.concatenate([high, low, high], axis=0))


def from_right(values, table):
    high, low = split(values)
    both = dot(high, table)
    return both[:, :PAD] + both[:, PAD:] + dot(low, table[:, :PAD])


def exchange_kernel(count, target_in, partners_in, forward_left, inverse_left, forward_right,
                    inverse_right, row_squares, lane_squares, slabs, vectors, gathered, one, two,
                    target, partners, done, send, receive, own_sem, load_sem, done_sem):
    group = 8
    me = lax.axis_index("band")
    loads = [
        pltpu.make_async_copy(target_in, target, load_sem.at[0]),
        pltpu.make_async_copy(partners_in, partners, load_sem.at[1]),
    ]
    for load in loads:
        load.start()
    barrier_all(me, count)

    def slab(step):
        other = lax.rem(me + step, count)
        return remote(slabs.at[other], gathered.at[me], send.at[step], receive.at[step], other)

    for step in range(1, count):
        slab(step).start()
    own = pltpu.make_async_copy(slabs.at[me], gathered.at[me], own_sem)
    own.start()
    for load in loads:
        load.wait()

    def ahead(step, carry):
        planes = pl.ds(step * group, group)
        left = target[planes].astype(jnp.float32)
        parts = []
        for r in range(NP):
            density = left * partners[r, planes].astype(jnp.float32)
            parts.append(from_right(density.reshape(group * NG, NG), forward_right[...]))
        values = jnp.concatenate(parts, axis=1).reshape(group, NG, NP * PAD)
        out = jnp.stack([from_left(forward_left[...], values[i]) for i in range(group)])
        one[:, pl.ds(pl.multiple_of(step * group, group), group), :] = jnp.swapaxes(out, 0, 1)
        return carry

    lax.fori_loop(0, NG // group, ahead, 0)

    def middle(step, carry):
        outs = []
        for i in range(group):
            number = step * group + i
            folded = jnp.where(number <= NG // 2, number, number - NG // 2)
            wave = (2.0 * np.pi / NG) * folded.astype(jnp.float32)
            totals = row_squares[...] + lane_squares[...] + wave * wave
            weight = jnp.where(totals > 0.0, 1.0 / (0.0025 + totals), 0.0)
            spectrum = from_left(forward_left[...], one[number]) * weight
            outs.append(from_left(inverse_left[...], spectrum))
        out = jnp.stack(outs)
        two[:, pl.ds(pl.multiple_of(step * group, group), group), :] = jnp.swapaxes(out, 0, 1)
        return carry

    lax.fori_loop(0, NG // group, middle, 0)

    def back(step, carry):
        planes = pl.ds(step * group, group)
        values = jnp.stack(
            [from_left(inverse_left[...], two[step * group + i]) for i in range(group)]
        ).reshape(group * NG, NP * PAD)
        total = jnp.zeros((group, NG, NG), jnp.float32)
        for r in range(NP):
            potential = from_right(values[:, r * PAD : (r + 1) * PAD], inverse_right[...])
            potential = potential.reshape(group, NG, PAD)[:, :, :NG]
            total -= partners[r, planes].astype(jnp.float32) * potential
        done[planes] = total
        stored(step).start()
        return carry

    def stored(step):
        planes = pl.ds(step * group, group)
        return pltpu.make_async_copy(done.at[planes], vectors.at[planes], done_sem.at[step])

    lax.fori_loop(0, NG // group, back, 0)
    for step in range(NG // group):
        stored(step).wait()
    own.wait()
    for step in range(1, count):
        slab(step).wait()


def exchange(target, partners, slabs, count):
    fourier, squares = tables(NG)
    lanes = np.zeros((PAD,), np.float32)
    lanes[:NG] = squares
    vmem = pl.BlockSpec(memory_space=pltpu.VMEM)
    anywhere = pl.BlockSpec(memory_space=pl.ANY)
    dma = pltpu.SemaphoreType.DMA
    return pl.pallas_call(
        functools.partial(exchange_kernel, count),
        out_shape=(
            jax.ShapeDtypeStruct((NG, NG, NG), jnp.float32),
            jax.ShapeDtypeStruct(slabs.shape, slabs.dtype),
        ),
        in_specs=[anywhere] * 2 + [vmem] * 6 + [anywhere],
        out_specs=(anywhere, anywhere),
        scratch_shapes=[pltpu.VMEM((NG, NG, NP * PAD), jnp.float32)] * 2
        + [
            pltpu.VMEM(target.shape, target.dtype),
            pltpu.VMEM(partners.shape, partners.dtype),
            pltpu.VMEM((NG, NG, NG), jnp.float32),
            dma((count,)), dma((count,)), dma, dma((2,)), dma((NG // 8,)),
        ],
        compiler_params=pltpu.CompilerParams(
            collective_id=2, has_side_effects=True, vmem_limit_bytes=60 << 20
        ),
        cost_estimate=pl.CostEstimate(
            flops=12 * NP * NG**4, bytes_accessed=8 << 20, transcendentals=0
        ),
        name="exchange",
    )(
        target,
        partners,
        left_table(fourier),
        left_table(fourier.T.copy()),
        right_table(fourier.T.copy(), NG),
        right_table(fourier, PAD),
        np.broadcast_to(squares[:, None], (NG, NP * PAD)).copy(),
        np.tile(lanes, NP)[None, :],
        slabs,
    )


def body(orbitals):
    devices = lax.axis_size("band")
    points = orbitals.shape[1]
    target, row = pick(orbitals)
    partners = share(row.reshape(QUARTERS, CHUNKS, -1, PAD), devices)
    vectors, target_slab = exchange(
        target.reshape(NG, NG, NG),
        partners.reshape(NP, NG, NG, NG),
        target.reshape(devices, 8, points // devices // 8),
        devices,
    )
    vector_slab = lax.all_to_all(
        vectors.reshape(1, points), "band", split_axis=1, concat_axis=0, tiled=True
    )
    target_slab = target_slab.reshape(devices, points // devices).astype(jnp.float32)
    part = jnp.einsum("ap,bp->ab", target_slab, vector_slab, precision=highest) / NG**3
    intersection = sum_all(part, devices)
    metric = -0.5 * (intersection + intersection.T)
    factor = lax.linalg.cholesky(metric, symmetrize_input=False)
    return jax.scipy.linalg.solve_triangular(factor, vector_slab, lower=True)


def solution(mesh):
    placed = (P(("spin", "band"), None),)
    return jax.shard_map(
        body, mesh=mesh, in_specs=placed, out_specs=P("spin", "band"), check_vma=False
    )
```

```python
import functools

import jax
import jax.numpy as jnp
import numpy as np
from jax import lax
from jax.experimental import pallas as pl
from jax.experimental.pallas import tpu as pltpu
from jax.sharding import PartitionSpec as P

NG = 80
NP = 2
PAD = 128
QUARTERS = 4
CHUNKS = 5
highest = lax.Precision.HIGHEST


def tables(length):
    indices = np.arange(length)
    nyquist = length // 2
    frequency = np.where(indices <= nyquist, indices, indices - nyquist)
    angles = 2.0 * np.pi / length * (frequency[:, None] * indices[None, :] % length)
    edges = (indices == 0) | (indices == nyquist)
    weights = np.where(edges, 1.0 / length, 2.0 / length)
    fourier = np.where((indices <= nyquist)[:, None], np.cos(angles), np.sin(angles))
    fourier = (fourier * np.sqrt(weights)[:, None]).astype(np.float32)
    squares = ((2.0 * np.pi / length * frequency) ** 2).astype(np.float32)
    return fourier, squares


def halves(table):
    high = table.astype(jnp.bfloat16)
    low = (table - high.astype(np.float32)).astype(jnp.bfloat16)
    return high, low


def left_table(table):
    high, low = halves(table)
    return np.concatenate([high, high, low], axis=1)


def right_table(table, depth):
    high, low = halves(table)
    result = np.zeros((depth, 2 * PAD), dtype=high.dtype)
    result[: table.shape[0], : table.shape[1]] = high
    result[: table.shape[0], PAD : PAD + table.shape[1]] = low
    return result


def barrier_all(me, count):
    barrier = pltpu.get_barrier_semaphore()
    for step in range(1, count):
        pl.semaphore_signal(
            barrier, inc=1, device_id={"band": lax.rem(me + step, count)},
            device_id_type=pl.DeviceIdType.MESH,
        )
    pl.semaphore_wait(barrier, count - 1)


def remote(source, target, send, receive, device):
    return pltpu.make_async_remote_copy(
        src_ref=source, dst_ref=target, send_sem=send, recv_sem=receive,
        device_id={"band": device}, device_id_type=pl.DeviceIdType.MESH,
    )


def share_kernel(count, row, partners, first_send, column_send, plane_send, receive, own_sem):
    me = lax.axis_index("band")
    planes = count // QUARTERS
    stride = count // NP
    column = lax.rem(me, QUARTERS)
    plane = lax.div(me, QUARTERS)
    base = plane * QUARTERS
    barrier_all(me, count)

    def first(r, q, c):
        return remote(row.at[q, c], partners.at[r, q, c], first_send.at[q - 1, c],
                      receive.at[r, q, c], lax.rem(me + q, count))

    def down(r, step, c):
        other = lax.rem(me + step * QUARTERS, count)
        return remote(partners.at[r, column, c], partners.at[r, column, c],
                      column_send.at[r, step - 1, c], receive.at[r, column, c], other)

    def neighbour(step):
        return base + lax.rem(column + step, QUARTERS)

    def across(r, step, c):
        return remote(partners.at[r, column, c], partners.at[r, column, c],
                      plane_send.at[r, step - 1, c], receive.at[r, column, c], neighbour(step))

    def arrived(r, q, c):
        remote(partners.at[r, q, c], partners.at[r, q, c], plane_send.at[r, 0, c],
               receive.at[r, q, c], me).wait_recv()

    for r in range(NP):
        @pl.when(me == r * stride)
        def _():
            own = pltpu.make_async_copy(row, partners.at[r], own_sem)
            own.start()
            own.wait()

    for c in range(CHUNKS):
        for r in range(NP):
            @pl.when(me != r * stride)
            def _():
                arrived(r, column, c)

            @pl.when(me == r * stride)
            def _():
                for q in range(1, QUARTERS):
                    first(r, q, c).start()

            @pl.when(plane == r * stride // QUARTERS)
            def _():
                for step in range(1, planes):
                    down(r, step, c).start()

            for step in range(1, QUARTERS):
                @pl.when(neighbour(step) != r * stride)
                def _():
                    across(r, step, c).start()

    for r in range(NP):
        @pl.when(me != r * stride)
        def _():
            for c in range(CHUNKS):
                for step in range(1, QUARTERS):
                    arrived(r, lax.rem(column + step, QUARTERS), c)

        @pl.when(me == r * stride)
        def _():
            for c in range(CHUNKS):
                for q in range(1, QUARTERS):
                    first(r, q, c).wait_send()

        @pl.when(plane == r * stride // QUARTERS)
        def _():
            for c in range(CHUNKS):
                for step in range(1, planes):
                    down(r, step, c).wait_send()

        for step in range(1, QUARTERS):
            @pl.when(neighbour(step) != r * stride)
            def _():
                for c in range(CHUNKS):
                    across(r, step, c).wait_send()


def share(row, count):
    planes = count // QUARTERS
    anywhere = pl.BlockSpec(memory_space=pl.ANY)
    dma = pltpu.SemaphoreType.DMA
    return pl.pallas_call(
        functools.partial(share_kernel, count),
        out_shape=jax.ShapeDtypeStruct((NP,) + row.shape, row.dtype),
        in_specs=[pl.BlockSpec(memory_space=pltpu.HBM)],
        out_specs=anywhere,
        scratch_shapes=[
            dma((QUARTERS - 1, CHUNKS)), dma((NP, planes - 1, CHUNKS)),
            dma((NP, QUARTERS - 1, CHUNKS)), dma((NP, QUARTERS, CHUNKS)), dma,
        ],
        compiler_params=pltpu.CompilerParams(
            collective_id=0, has_side_effects=True, vmem_limit_bytes=1 << 20
        ),
        name="share",
    )(row)


def sum_kernel(count, part, total, held, send, receive):
    me = lax.axis_index("band")
    barrier_all(me, count)

    def copy(step):
        return remote(part, held.at[step], send.at[step], receive.at[step],
                      lax.rem(me + step, count))

    for step in range(1, count):
        copy(step).start()
    held[0] = part[...]
    for step in range(1, count):
        copy(step).wait()
    total[...] = jnp.sum(held[...], axis=0)


def sum_all(part, count):
    vmem = pl.BlockSpec(memory_space=pltpu.VMEM)
    return pl.pallas_call(
        functools.partial(sum_kernel, count),
        out_shape=jax.ShapeDtypeStruct(part.shape, jnp.float32),
        in_specs=[vmem],
        out_specs=vmem,
        scratch_shapes=[
            pltpu.VMEM((count,) + part.shape, jnp.float32),
            pltpu.SemaphoreType.DMA((count,)),
            pltpu.SemaphoreType.DMA((count,)),
        ],
        compiler_params=pltpu.CompilerParams(
            collective_id=1, has_side_effects=True, vmem_limit_bytes=4 << 20
        ),
        name="sum_all",
    )(part)


def pick_kernel(orbitals, first, last):
    owned, width = orbitals.shape
    values = orbitals[...].astype(jnp.float32)
    first[...] = values[0:1].reshape(width // PAD, PAD).astype(first.dtype)
    last[...] = values[owned - 1 : owned].reshape(width // PAD, PAD).astype(last.dtype)


def pick(orbitals):
    owned, points = orbitals.shape
    steps = 10
    width = points // steps
    row = jax.ShapeDtypeStruct((points // PAD, PAD), orbitals.dtype)
    spec = pl.BlockSpec((width // PAD, PAD), lambda i: (i, 0))
    return pl.pallas_call(
        pick_kernel,
        grid=(steps,),
        out_shape=(row, row),
        in_specs=[pl.BlockSpec((owned, width), lambda i: (0, i))],
        out_specs=(spec, spec),
        compiler_params=pltpu.CompilerParams(vmem_limit_bytes=6 << 20),
        name="pick",
    )(orbitals)


def split(values):
    high = values.astype(jnp.bfloat16)
    low = (values - high.astype(jnp.float32)).astype(jnp.bfloat16)
    return high, low


def dot(left, right):
    return lax.dot_general(left, right, (((1,), (0,)), ((), ())),
                           preferred_element_type=jnp.float32)


def from_left(table, values):
    high, low = split(values)
    return dot(table, jnp.concatenate([high, low, high], axis=0))


def from_right(values, table):
    high, low = split(values)
    both = dot(high, table)
    return both[:, :PAD] + both[:, PAD:] + dot(low, table[:, :PAD])


def exchange_kernel(count, target_in, partners_in, forward_left, inverse_left, forward_right,
                    inverse_right, row_squares, lane_squares, slabs, vectors, gathered, one, two,
                    target, partners, done, send, receive, own_sem, load_sem, done_sem):
    group = 8
    me = lax.axis_index("band")
    loads = [
        pltpu.make_async_copy(target_in, target, load_sem.at[0]),
        pltpu.make_async_copy(partners_in, partners, load_sem.at[1]),
    ]
    for load in loads:
        load.start()
    barrier_all(me, count)

    def slab(step):
        other = lax.rem(me + step, count)
        return remote(slabs.at[other], gathered.at[me], send.at[step], receive.at[step], other)

    for step in range(1, count):
        slab(step).start()
    own = pltpu.make_async_copy(slabs.at[me], gathered.at[me], own_sem)
    own.start()
    for load in loads:
        load.wait()

    def ahead(step, carry):
        planes = pl.ds(step * group, group)
        left = target[planes].astype(jnp.float32)
        parts = []
        for r in range(NP):
            density = left * partners[r, planes].astype(jnp.float32)
            parts.append(from_right(density.reshape(group * NG, NG), forward_right[...]))
        values = jnp.concatenate(parts, axis=1).reshape(group, NG, NP * PAD)
        out = jnp.stack([from_left(forward_left[...], values[i]) for i in range(group)])
        one[:, pl.ds(pl.multiple_of(step * group, group), group), :] = jnp.swapaxes(out, 0, 1)
        return carry

    lax.fori_loop(0, NG // group, ahead, 0)

    def middle(step, carry):
        outs = []
        for i in range(group):
            number = step * group + i
            folded = jnp.where(number <= NG // 2, number, number - NG // 2)
            wave = (2.0 * np.pi / NG) * folded.astype(jnp.float32)
            totals = row_squares[...] + lane_squares[...] + wave * wave
            weight = jnp.where(totals > 0.0, 1.0 / (0.0025 + totals), 0.0)
            spectrum = from_left(forward_left[...], one[number]) * weight
            outs.append(from_left(inverse_left[...], spectrum))
        out = jnp.stack(outs)
        two[:, pl.ds(pl.multiple_of(step * group, group), group), :] = jnp.swapaxes(out, 0, 1)
        return carry

    lax.fori_loop(0, NG // group, middle, 0)

    def back(step, carry):
        planes = pl.ds(step * group, group)
        values = jnp.stack(
            [from_left(inverse_left[...], two[step * group + i]) for i in range(group)]
        ).reshape(group * NG, NP * PAD)
        total = jnp.zeros((group, NG, NG), jnp.float32)
        for r in range(NP):
            potential = from_right(values[:, r * PAD : (r + 1) * PAD], inverse_right[...])
            potential = potential.reshape(group, NG, PAD)[:, :, :NG]
            total -= partners[r, planes].astype(jnp.float32) * potential
        done[planes] = total
        stored(step).start()
        return carry

    def stored(step):
        planes = pl.ds(step * group, group)
        return pltpu.make_async_copy(done.at[planes], vectors.at[planes], done_sem.at[step])

    lax.fori_loop(0, NG // group, back, 0)
    for step in range(NG // group):
        stored(step).wait()
    own.wait()
    for step in range(1, count):
        slab(step).wait()


def exchange(target, partners, slabs, count):
    fourier, squares = tables(NG)
    lanes = np.zeros((PAD,), np.float32)
    lanes[:NG] = squares
    vmem = pl.BlockSpec(memory_space=pltpu.VMEM)
    anywhere = pl.BlockSpec(memory_space=pl.ANY)
    dma = pltpu.SemaphoreType.DMA
    return pl.pallas_call(
        functools.partial(exchange_kernel, count),
        out_shape=(
            jax.ShapeDtypeStruct((NG, NG, NG), jnp.float32),
            jax.ShapeDtypeStruct(slabs.shape, slabs.dtype),
        ),
        in_specs=[anywhere] * 2 + [vmem] * 6 + [anywhere],
        out_specs=(anywhere, anywhere),
        scratch_shapes=[pltpu.VMEM((NG, NG, NP * PAD), jnp.float32)] * 2
        + [
            pltpu.VMEM(target.shape, target.dtype),
            pltpu.VMEM(partners.shape, partners.dtype),
            pltpu.VMEM((NG, NG, NG), jnp.float32),
            dma((count,)), dma((count,)), dma, dma((2,)), dma((NG // 8,)),
        ],
        compiler_params=pltpu.CompilerParams(
            collective_id=2, has_side_effects=True, vmem_limit_bytes=60 << 20
        ),
        cost_estimate=pl.CostEstimate(
            flops=12 * NP * NG**4, bytes_accessed=8 << 20, transcendentals=0
        ),
        name="exchange",
    )(
        target,
        partners,
        left_table(fourier),
        left_table(fourier.T.copy()),
        right_table(fourier.T.copy(), NG),
        right_table(fourier, PAD),
        np.broadcast_to(squares[:, None], (NG, NP * PAD)).copy(),
        np.tile(lanes, NP)[None, :],
        slabs,
    )


def body(orbitals):
    devices = lax.axis_size("band")
    points = orbitals.shape[1]
    target, row = pick(orbitals)
    partners = share(row.reshape(QUARTERS, CHUNKS, -1, PAD), devices)
    vectors, target_slab = exchange(
        target.reshape(NG, NG, NG),
        partners.reshape(NP, NG, NG, NG),
        target.reshape(devices, 8, points // devices // 8),
        devices,
    )
    vector_slab = lax.all_to_all(
        vectors.reshape(1, points), "band", split_axis=1, concat_axis=0, tiled=True
    )
    target_slab = target_slab.reshape(devices, points // devices).astype(jnp.float32)
    part = jnp.einsum("ap,bp->ab", target_slab, vector_slab, precision=highest) / NG**3
    intersection = sum_all(part, devices)
    metric = -0.5 * (intersection + intersection.T)
    factor = lax.linalg.cholesky(metric, symmetrize_input=False)
    return jax.scipy.linalg.solve_triangular(factor, vector_slab, lower=True)


def solution(mesh):
    placed = (P(("spin", "band"), None),)
    return jax.shard_map(
        body, mesh=mesh, in_specs=placed, out_specs=P("spin", "band"), check_vma=False
    )
```
